512 devices in a mesh: dom: 128 (over z, y, core), sub: 4 (over x).
Axes of the slice: x: 4, y: 8, z: 8, core: 2. Of those that a mesh axis runs over, the one named last changes fastest.
Arguments:
- source: float32 [512, 7, 16, 1024], P('dom', None, 'sub'), may hold values from -6 to 6
- zone_ids: int32 [512, 1024], P('dom'), may hold values from 0 to 15
- kappa_table: float32 [16, 7], replicated, may hold values from 0.05 to 1
- mu_table: float32 [16, 8], replicated, may hold values from 0.2 to 2
- owner_dev: int32 [128, 32], P('dom'), may hold values from 0 to 127, as said below
- owner_group: int32 [128, 128], P('dom'), may hold values from 0 to 127, as said below
Outputs:
- edge_field: float32 [512, 7, 16, 1024], P('dom', None, 'sub')
- potential: float32 [512, 16, 1024], P('dom', 'sub')
The draws below stay inside these ranges and needn't reach their ends.
Inputs may be any that keep to these rules, and one draw needn't show every extreme that they name: owner_dev[d, j] is the index along dom of the device that sums slot j of device d; one device sends at most 1 of its slots to one owner, and exactly 1 to some owner. At owner e, receive position d + c stands for the c-th slot, in slot order, that device d sends to e. owner_group[e, d + c] is a receive position held alike by all copies of one shared primitive; a primitive has at most four copies, all at one owner; positions that no slot reaches hold their own index.
All inputs are finite; a program needn't handle non-finite values.
Results may differ from the reference program's by a relative error of at most 0.0001.
Values sent between devices are 32-bit elements; how exact they have to be, the bound alone decides.
A program may use at most 64 MiB of HBM per device.

```python
import math
import jax
import jax.numpy as jnp
from jax import lax

MACROS = 4
LAT = 32
ZONES = 16
SWEEPS = 2
CELLS = 1024
SLOTS = 32
CAP = 1
RECV = 128
MACRO_ALL = 512
DEPTH = 16
N_DOM = 128
N_SUB = 4


def layout(key):
    base_key = jax.random.fold_in(key, 4177)
    slot_key, peer_key, score_key = jax.random.split(base_key, 3)
    slot_orders = jax.vmap(lambda item_key: jax.random.permutation(item_key, SLOTS))(jax.random.split(slot_key, N_DOM))
    peer_orders = jax.vmap(lambda item_key: jax.random.permutation(item_key, N_DOM))(jax.random.split(peer_key, N_DOM))
    owners = jnp.take_along_axis(peer_orders, slot_orders % N_DOM, axis=1).astype(jnp.int32)
    earlier = jnp.arange(SLOTS)[None, :] < jnp.arange(SLOTS)[:, None]
    same_owner = owners[:, :, None] == owners[:, None, :]
    position = jnp.sum(same_owner & earlier[None], axis=2).astype(jnp.int32)
    receive = jnp.arange(N_DOM, dtype=jnp.int32)[:, None] * CAP + position
    flat_index = (owners * RECV + receive).reshape(-1)
    live = jnp.zeros((N_DOM * RECV,), jnp.int32).at[flat_index].set(1).reshape(N_DOM, RECV)
    random_part = jax.random.randint(score_key, (N_DOM, RECV), 0, 32768).astype(jnp.int32)
    index_row = jnp.arange(RECV, dtype=jnp.int32)[None, :]
    scores = jnp.where(live > 0, random_part * RECV + index_row, 1073741824 + index_row)
    order = jnp.argsort(scores, axis=1).astype(jnp.int32)
    ranks = jnp.argsort(order, axis=1).astype(jnp.int32)
    live_count = jnp.sum(live, axis=1, keepdims=True)
    quad_end = 4 * (live_count // 8)
    leader_rank = jnp.where(ranks < quad_end, ranks - ranks % 4, ranks - ranks % 2)
    leaders = jnp.take_along_axis(order, leader_rank, axis=1)
    groups = jnp.where(live > 0, leaders, index_row).astype(jnp.int32)
    return (owners, groups)


def draw_owner_dev(key, part):
    owners, groups = layout(key)
    return owners


def draw_owner_group(key, part):
    owners, groups = layout(key)
    return groups


def place_ends(values, stream_key, low, top_value):
    extent = values.shape
    index_at = [jax.random.randint(jax.random.fold_in(stream_key, axis), (), 0, extent[axis]) for axis in range(len(extent))]
    values = values.at[tuple(index_at)].set(low)
    longest = extent.index(max(extent))
    index_at[longest] = (index_at[longest] + 1) % extent[longest]
    return values.at[tuple(index_at)].set(top_value)


def shard_levels(own_key, shape, cuts, smallest, largest):
    level = 1.0
    for dim, blocks in cuts:
        heights = jax.random.uniform(jax.random.fold_in(jax.random.fold_in(own_key, 6), dim), (blocks,), jnp.float32, smallest / len(cuts), largest / len(cuts))
        level = level * jnp.repeat(jnp.exp(heights), shape[dim] // blocks).reshape((-1,) + (1,) * (len(shape) - 1 - dim))
    return level


def scatter_about(rng, extent, spread, reach, cuts=(), kind=jnp.bfloat16):
    loudness = shard_levels(rng, extent, cuts, -0.22, 0.18) if cuts else 1.0
    drawn = jax.random.normal(rng, extent, jnp.float32) * spread * loudness
    return jnp.minimum(jnp.maximum(drawn, -reach), reach).astype(kind)


def setup_inputs(seed: int = 0) -> dict:
    splits = jax.random.split(jax.random.key(seed), 7)
    source = scatter_about(splits[0], (MACRO_ALL, 7, DEPTH, CELLS), 1.0, 6.0, ((0, 128), (2, 4)), jnp.float32)
    zone_ids = place_ends(jax.random.randint(splits[1], (MACRO_ALL, CELLS), 0, ZONES), jax.random.fold_in(splits[1], 1), 0, ZONES - 1).astype(jnp.int32)
    kappa_table = jnp.clip(jnp.exp(jax.random.uniform(splits[2], (ZONES, 7), jnp.float32, math.log(0.05), math.log(1.0))), 0.05, 1.0)
    mu_table = jnp.clip(jnp.exp(jax.random.uniform(splits[3], (ZONES, 8), jnp.float32, math.log(0.2), math.log(2.0))), 0.2, 2.0)
    owner_dev = draw_owner_dev(jax.random.fold_in(splits[6], 71), 0)
    owner_group = draw_owner_group(jax.random.fold_in(splits[6], 71), 0)
    return {"source": source, "zone_ids": zone_ids, "kappa_table": kappa_table, "mu_table": mu_table, "owner_dev": owner_dev, "owner_group": owner_group}


EDGE_OFFSETS = ((0, 0, 1), (0, 1, 0), (1, 0, 0), (0, 1, 1), (1, 0, 1), (1, 1, 0), (1, 1, 1))
FACE_EDGES = ((0, 1, 3), (1, 0, 3), (0, 2, 4), (2, 0, 4), (1, 2, 5), (2, 1, 5), (3, 2, 6), (2, 3, 6))
SHARED_TYPES = (1, 2, 5)
EDGE_DAMPING = 0.6
NODE_DAMPING = 0.8


def shift_ahead(values, rise_y, rise_x):
    offset = rise_y * LAT + rise_x
    if offset == 0:
        return values
    padding = jnp.zeros(values.shape[:-1] + (offset,), values.dtype)
    shifted = jnp.concatenate([values[..., offset:], padding], axis=-1)
    if rise_x:
        column = jnp.arange(values.shape[-1]) % LAT
        shifted = jnp.where(column < LAT - rise_x, shifted, jnp.zeros_like(shifted))
    return shifted


def shift_behind(values, rise_y, rise_x):
    offset = rise_y * LAT + rise_x
    if offset == 0:
        return values
    padding = jnp.zeros(values.shape[:-1] + (offset,), values.dtype)
    shifted = jnp.concatenate([padding, values[..., :-offset]], axis=-1)
    if rise_x:
        column = jnp.arange(values.shape[-1]) % LAT
        shifted = jnp.where(column >= rise_x, shifted, jnp.zeros_like(shifted))
    return shifted


def apply_operator(padded, halo_width, extra_planes, first_plane, mass_coef, curl_coef):
    planes = padded.shape[2] - 2 * halo_width
    face_count = planes + extra_planes + 1
    first_face = halo_width - extra_planes - 1
    face_planes = first_plane - extra_planes - 1 + jnp.arange(face_count)
    face_valid = (face_planes >= 0)[None, :, None]
    result = [mass_coef[edge_type][:, None, :] * padded[:, edge_type, halo_width - extra_planes:halo_width + planes] for edge_type in range(7)]
    for face_index, (first_edge, second_edge, diagonal_edge) in enumerate(FACE_EDGES):
        rise_z, rise_y, rise_x = EDGE_OFFSETS[first_edge]
        far_values = shift_ahead(padded[:, second_edge, first_face + rise_z:first_face + rise_z + face_count], rise_y, rise_x)
        circulation = padded[:, first_edge, first_face:first_face + face_count] + far_values - padded[:, diagonal_edge, first_face:first_face + face_count]
        weighted = jnp.where(face_valid, curl_coef[face_index][:, None, :] * circulation, 0.0)
        result[first_edge] = result[first_edge] + weighted[:, 1:]
        result[diagonal_edge] = result[diagonal_edge] - weighted[:, 1:]
        result[second_edge] = result[second_edge] + shift_behind(weighted[:, 1 - rise_z:1 - rise_z + planes + extra_planes], rise_y, rise_x)
    return jnp.stack(result, axis=1)


def edge_diagonal(mass_coef, curl_coef, first_plane, planes):
    inside = ((first_plane + jnp.arange(planes)) >= 1)[None, :, None]
    flat_planes = jnp.zeros((1, planes, 1), mass_coef.dtype)
    diagonal = [mass_coef[edge_type][:, None, :] + flat_planes for edge_type in range(7)]
    for face_index, (first_edge, second_edge, diagonal_edge) in enumerate(FACE_EDGES):
        rise_z, rise_y, rise_x = EDGE_OFFSETS[first_edge]
        own_term = curl_coef[face_index][:, None, :]
        diagonal[first_edge] = diagonal[first_edge] + own_term
        diagonal[diagonal_edge] = diagonal[diagonal_edge] + own_term
        behind_term = shift_behind(curl_coef[face_index], rise_y, rise_x)[:, None, :] + flat_planes
        if rise_z:
            behind_term = jnp.where(inside, behind_term, 0.0)
        diagonal[second_edge] = diagonal[second_edge] + behind_term
    return jnp.stack(diagonal, axis=1)


def node_diagonal(mass_coef, first_plane, planes):
    inside = ((first_plane + jnp.arange(planes)) >= 1)[None, :, None]
    total = jnp.zeros((mass_coef.shape[1], planes, mass_coef.shape[2]), mass_coef.dtype)
    for edge_type in range(7):
        rise_z, rise_y, rise_x = EDGE_OFFSETS[edge_type]
        total = total + mass_coef[edge_type][:, None, :]
        behind_term = shift_behind(mass_coef[edge_type], rise_y, rise_x)[:, None, :] + jnp.zeros((1, planes, 1), mass_coef.dtype)
        if rise_z:
            behind_term = jnp.where(inside, behind_term, 0.0)
        total = total + behind_term
    return total


def node_residual(lowered, planes):
    total = jnp.zeros((lowered.shape[0], planes, lowered.shape[3]), lowered.dtype)
    for edge_type in range(7):
        rise_z, rise_y, rise_x = EDGE_OFFSETS[edge_type]
        total = total + shift_behind(lowered[:, edge_type, 1 - rise_z:1 - rise_z + planes], rise_y, rise_x) - lowered[:, edge_type, 1:]
    return total


def gradient(raised, planes):
    result = []
    for edge_type in range(7):
        rise_z, rise_y, rise_x = EDGE_OFFSETS[edge_type]
        result.append(shift_ahead(raised[:, rise_z:rise_z + planes], rise_y, rise_x) - raised[:, :planes])
    return jnp.stack(result, axis=1)


def edge_sides(values, layers):
    macro_count, type_count, plane_count, cell_count = values.shape
    lattice = values.reshape(macro_count, type_count, plane_count, LAT, LAT)
    chosen = jnp.stack([lattice[:, edge_type] for edge_type in SHARED_TYPES], axis=1)
    sides = jnp.stack([chosen[..., 0], chosen[..., LAT - 1]], axis=1)
    sides = jnp.transpose(sides, (0, 1, 3, 2, 4))
    sides = sides.reshape(macro_count, 2, layers, plane_count // layers, 3 * LAT)
    return jnp.transpose(sides, (2, 0, 1, 3, 4)).reshape(layers, -1, 3 * LAT)


def insert_edges(values, blocks, layers):
    macro_count, type_count, plane_count, cell_count = values.shape
    shaped = blocks.reshape(layers, macro_count, 2, plane_count // layers, 3, LAT)
    shaped = jnp.transpose(shaped, (1, 2, 4, 0, 3, 5)).reshape(macro_count, 2, 3, plane_count, LAT)
    lattice = values.reshape(macro_count, type_count, plane_count, LAT, LAT)
    for side_index, column in ((0, 0), (1, LAT - 1)):
        for slot_type, edge_type in enumerate(SHARED_TYPES):
            lattice = lattice.at[:, edge_type, :, :, column].set(shaped[:, side_index, slot_type])
    return lattice.reshape(values.shape)


def node_sides(values, layers):
    macro_count, plane_count, cell_count = values.shape
    lattice = values.reshape(macro_count, plane_count, LAT, LAT)
    sides = jnp.stack([lattice[..., 0], lattice[..., LAT - 1]], axis=1)
    sides = sides.reshape(macro_count, 2, layers, plane_count // layers, LAT)
    return jnp.transpose(sides, (2, 0, 1, 3, 4)).reshape(layers, -1, LAT)


def insert_nodes(values, blocks, layers):
    macro_count, plane_count, cell_count = values.shape
    shaped = blocks.reshape(layers, macro_count, 2, plane_count // layers, LAT)
    shaped = jnp.transpose(shaped, (1, 2, 0, 3, 4)).reshape(macro_count, 2, plane_count, LAT)
    lattice = values.reshape(macro_count, plane_count, LAT, LAT)
    for side_index, column in ((0, 0), (1, LAT - 1)):
        lattice = lattice.at[:, :, :, column].set(shaped[:, side_index])
    return lattice.reshape(values.shape)


def group_keys(owners, groups, capacity):
    device_count, slot_count = owners.shape
    earlier = jnp.arange(slot_count)[None, :] < jnp.arange(slot_count)[:, None]
    same_owner = owners[:, :, None] == owners[:, None, :]
    position = jnp.sum(same_owner & earlier[None], axis=2).astype(jnp.int32)
    receive = jnp.arange(device_count).astype(jnp.int32)[:, None] * capacity + position
    leaders = groups[owners, receive].astype(jnp.int32)
    return (owners * groups.shape[1] + leaders).astype(jnp.int32)


def assemble(blocks, keys):
    layers = blocks.shape[1]
    flattened = jnp.transpose(blocks, (1, 0, 2, 3)).reshape(layers, -1, blocks.shape[3])
    key_list = keys.reshape(-1)
    group_sums = jax.vmap(lambda layer_blocks: jax.ops.segment_sum(layer_blocks, key_list, N_DOM * RECV))(flattened)
    picked = group_sums[:, key_list]
    return jnp.transpose(picked.reshape(layers, N_DOM, -1, blocks.shape[3]), (1, 0, 2, 3))


def reference(source, zone_ids, kappa_table, mu_table, owner_dev, owner_group):
    fields = source.reshape(N_DOM, MACROS, 7, DEPTH, CELLS)
    zone_rows = zone_ids.reshape(N_DOM, MACROS, CELLS)
    keys = group_keys(owner_dev, owner_group, CAP)

    def lookup(zone_row):
        return jnp.moveaxis(kappa_table[zone_row], -1, 0), jnp.moveaxis(mu_table[zone_row], -1, 0)

    def operator_of(items):
        edge_values, zone_row = items
        mass_coef, curl_coef = lookup(zone_row)
        padded = jnp.pad(edge_values, ((0, 0), (0, 0), (1, 1), (0, 0)))
        return apply_operator(padded, 1, 0, 0, mass_coef, curl_coef)

    def diagonal_blocks(zone_row):
        mass_coef, curl_coef = lookup(zone_row)
        return edge_sides(edge_diagonal(mass_coef, curl_coef, 0, DEPTH), N_SUB), node_sides(node_diagonal(mass_coef, 0, DEPTH), N_SUB)

    edge_diag_blocks, node_diag_blocks = lax.map(diagonal_blocks, zone_rows)
    edge_diag_sum = assemble(edge_diag_blocks, keys)
    node_diag_sum = assemble(node_diag_blocks, keys)

    def edge_step(items):
        edge_values, residual_values, zone_row, residual_blocks, diag_blocks = items
        mass_coef, curl_coef = lookup(zone_row)
        full_residual = insert_edges(residual_values, residual_blocks, N_SUB)
        full_diagonal = insert_edges(edge_diagonal(mass_coef, curl_coef, 0, DEPTH), diag_blocks, N_SUB)
        return edge_values + EDGE_DAMPING * full_residual / full_diagonal

    def node_step(items):
        edge_values, source_values, zone_row = items
        residual_new = source_values - operator_of((edge_values, zone_row))
        lowered = jnp.pad(residual_new, ((0, 0), (0, 0), (1, 0), (0, 0)))
        return node_residual(lowered, DEPTH)

    def potential_step(items):
        node_values, zone_row, node_blocks, diag_blocks = items
        mass_coef, curl_coef = lookup(zone_row)
        full_nodes = insert_nodes(node_values, node_blocks, N_SUB)
        full_diagonal = insert_nodes(node_diagonal(mass_coef, 0, DEPTH), diag_blocks, N_SUB)
        return NODE_DAMPING * full_nodes / full_diagonal

    def raise_step(items):
        edge_values, correction_values = items
        raised = jnp.pad(correction_values, ((0, 0), (0, 1), (0, 0)))
        return edge_values + gradient(raised, DEPTH)

    edge_field = jnp.zeros_like(fields)
    potential = jnp.zeros((N_DOM, MACROS, DEPTH, CELLS), fields.dtype)
    for sweep_index in range(SWEEPS):
        if sweep_index == 0:
            residual = fields
        else:
            residual = fields - lax.map(operator_of, (edge_field, zone_rows))
        residual_sum = assemble(lax.map(lambda items: edge_sides(items, N_SUB), residual), keys)
        edge_field = lax.map(edge_step, (edge_field, residual, zone_rows, residual_sum, edge_diag_sum))
        node_values = lax.map(node_step, (edge_field, fields, zone_rows))
        node_sum = assemble(lax.map(lambda items: node_sides(items, N_SUB), node_values), keys)
        correction = lax.map(potential_step, (node_values, zone_rows, node_sum, node_diag_sum))
        edge_field = lax.map(raise_step, (edge_field, correction))
        potential = potential + correction
    return edge_field.reshape(MACRO_ALL, 7, DEPTH, CELLS), potential.reshape(MACRO_ALL, DEPTH, CELLS)
```

```python
import functools

import jax
import jax.numpy as jnp
from jax import lax
from jax.experimental import pallas as pl
from jax.experimental.pallas import tpu as pltpu
from jax.sharding import PartitionSpec as P

MESH = pl.DeviceIdType.MESH
LAT = 32
PLANES = 4
CORES = 2
EDGE_DAMPING = 0.6
NODE_DAMPING = 0.8
POS = {0: 0, 1: 1, 3: 2, 2: 3, 4: 4, 5: 5, 6: 6}
FLAT_TYPES = (0, 1, 3)
SHARED = (1, 2, 5)
PRIVATE = (0, 3, 4, 6)
TILE = (8, 128)


class Lanes:
    def __init__(self):
        self.lane = lax.broadcasted_iota(jnp.int32, TILE, 1)
        self.sub = lax.broadcasted_iota(jnp.int32, TILE, 0)
        self.x = self.lane % LAT
        self.left = self.x == 0
        self.right = self.x == LAT - 1
        self.last_y = (self.sub == 7) & (self.lane >= 96)
        self.first_y = (self.sub == 0) & (self.lane < 32)

    def side(self, s):
        return self.right if s else self.left

    def ax(self, v):
        return jnp.where(self.right, 0.0, pltpu.roll(v, 127, 1))

    def bx(self, v):
        return jnp.where(self.left, 0.0, pltpu.roll(v, 1, 1))

    def ay(self, v):
        r = pltpu.roll(v, 96, 1)
        r = jnp.where(self.lane < 96, r, pltpu.roll(r, 7, 0))
        return jnp.where(self.last_y, 0.0, r)

    def by(self, v):
        r = pltpu.roll(v, 32, 1)
        r = jnp.where(self.lane >= 32, r, pltpu.roll(r, 1, 0))
        return jnp.where(self.first_y, 0.0, r)

    def pack(self, v, s, idx):
        return pltpu.roll(jnp.where(self.side(s), v, 0.0), (idx - s * (LAT - 1) + 128) % 128, 1)

    def unpack(self, v, s, idx):
        return pltpu.roll(v, (s * (LAT - 1) - idx + 128) % 128, 1)


class Gather:
    def __init__(self, buf, sems, me, side):
        self.buf, self.sems = buf, sems
        self.side = side
        self.core, self.a, self.b, self.k, self.dev = me
        self.sent = []

    def row(self):
        return (self.core * self.side + self.a) * self.side + self.b

    def line(self, core, a):
        return self.buf.at[pl.ds((core * self.side + a) * self.side, self.side)]

    def send(self, stage, i, ref, target):
        copy = pltpu.make_async_remote_copy(
            src_ref=ref,
            dst_ref=ref,
            send_sem=self.sems.at[stage, 0, i],
            recv_sem=self.sems.at[stage, 1, i],
            device_id=target,
            device_id_type=MESH,
        )
        copy.start()
        self.sent.append(copy)

    def arrived(self, stage, i, ref):
        pltpu.make_async_remote_copy(
            src_ref=ref,
            dst_ref=ref,
            send_sem=self.sems.at[stage, 0, i],
            recv_sem=self.sems.at[stage, 1, i],
            device_id=self.dev(self.core, self.a, self.b),
            device_id_type=MESH,
        ).wait_recv()

    def first(self):
        ref = self.buf.at[self.row()]
        for i in range(1, self.side):
            self.send(0, i, ref, self.dev(self.core, self.a, (self.b + i) % self.side))

    def second(self):
        for i in range(1, self.side):
            source = (self.b - i + self.side) % self.side
            self.arrived(0, i, self.buf.at[(self.core * self.side + self.a) * self.side + source])
        ref = self.line(self.core, self.a)
        for i in range(1, self.side):
            self.send(1, i, ref, self.dev(self.core, (self.a + i) % self.side, self.b))
        self.send(2, 0, ref, self.dev(1 - self.core, self.b, self.a))

    def third(self):
        for i in range(1, self.side):
            ref = self.line(self.core, (self.a - i + self.side) % self.side)
            self.arrived(1, i, ref)
            self.send(2, i, ref, self.dev(1 - self.core, self.b, self.a))

    def finish(self):
        for i in range(self.side):
            self.arrived(2, i, self.line(1 - self.core, (self.b - i + self.side) % self.side))

    def drain(self):
        for copy in self.sent:
            copy.wait_send()


def kernel(
    side, n_sub, macros, zones,
    src, zone, od_s, od_v, og_v, kappa, mu,
    out_e, out_p,
    S, EF, R, SB, SA, RB, RA, NR, NB, NA, C1, C2,
    MC, INVH, INV0, INVS, NDH, ND0, ND,
    G0, G1, G2, G3, GI, HS, HR,
    ODS, GRS, JS, IDXV, IDXS,
    gsem, bsem, hsem, isem,
):
    dom = lax.axis_index("dom")
    k = lax.axis_index("sub")
    core = dom % CORES
    zc = dom // (CORES * side)
    yc = (dom // CORES) % side
    a = jnp.where(core == 0, zc, yc)
    b = jnp.where(core == 0, yc, zc)

    def dev(core_, a_, b_):
        z_ = jnp.where(core_ == 0, a_, b_)
        y_ = jnp.where(core_ == 0, b_, a_)
        return ((z_ * side + y_) * CORES + core_, k)

    me = (core, a, b, k, dev)
    barrier = pltpu.get_barrier_semaphore()

    def greet(target):
        pl.semaphore_signal(barrier, inc=1, device_id=target, device_id_type=MESH)

    for i in range(1, side):
        greet(dev(core, a, (b + i) % side))
        greet(dev(core, (a + i) % side, b))
    greet(dev(1 - core, b, a))
    has_up = k < n_sub - 1
    has_down = k > 0

    @pl.when(has_up)
    def _():
        greet((dom, k + 1))

    @pl.when(has_down)
    def _():
        greet((dom, k - 1))

    ln = Lanes()
    ahead = {0: ln.ax, 1: ln.ay, 3: lambda v: ln.ax(ln.ay(v))}
    behind = {0: ln.bx, 1: ln.by, 3: lambda v: ln.bx(ln.by(v))}
    zero = jnp.zeros(TILE, jnp.float32)
    inside0 = jnp.where(has_down, 1.0, 0.0)

    nd_dev = side * side * CORES
    for buf in (G0, G1, G2, G3):
        for u in range(buf.shape[1]):
            buf[nd_dev, u] = zero

    gi = Gather(GI, gsem.at[4], me, side)
    g0 = Gather(G0, gsem.at[0], me, side)
    g1 = Gather(G1, gsem.at[1], me, side)
    g2 = Gather(G2, gsem.at[2], me, side)
    g3 = Gather(G3, gsem.at[3], me, side)
    row = gi.row()

    GI[row] = jnp.full(TILE, -1, jnp.int32)
    GI[row, 0:1, 0 : og_v.shape[1]] = og_v[...]
    GI[row, 1:2, 0 : od_v.shape[1]] = od_v[...]

    def prepare(m, packs):
        zid = zone[m]
        hits = [zid == zz for zz in range(zones)]
        mass, curl = [], []
        for t in range(7):
            v = zero
            for zz in range(zones):
                v = jnp.where(hits[zz], kappa[t, zz], v)
            mass.append(v)
            MC[m, t] = v
        for f in range(8):
            v = zero
            for zz in range(zones):
                v = jnp.where(hits[zz], mu[f, zz], v)
            curl.append(v)
            MC[m, 7 + f] = v
        diag = {
            0: mass[0] + curl[0] + curl[2] + behind[1](curl[1]),
            1: mass[1] + curl[1] + curl[4] + behind[0](curl[0]),
            2: mass[2] + curl[3] + curl[5] + curl[7] + behind[0](curl[2]) + behind[1](curl[4]) + behind[3](curl[6]),
            3: mass[3] + curl[0] + curl[1] + curl[6],
            4: mass[4] + curl[2] + curl[3],
            5: mass[5] + curl[4] + curl[5],
            6: mass[6] + curl[6] + curl[7],
        }
        low = {0: curl[3], 1: curl[5], 3: curl[7]}
        node = functools.reduce(lambda p, q: p + q, mass) + behind[0](mass[0]) + behind[1](mass[1]) + behind[3](mass[3])
        node_low = mass[2] + behind[0](mass[4]) + behind[1](mass[5]) + behind[3](mass[6])
        full = {t: diag[t] + low[t] if t in low else diag[t] for t in range(7)}
        first = {t: diag[t] + inside0 * low[t] if t in low else diag[t] for t in range(7)}
        for t in range(7):
            INVH[m, POS[t]] = EDGE_DAMPING / full[t]
        for n, t in enumerate(FLAT_TYPES):
            INV0[m, n] = EDGE_DAMPING / first[t]
        for n, t in enumerate(SHARED):
            INVS[m, n, 0] = first[t]
            for p in range(1, PLANES):
                INVS[m, n, p] = full[t]
        node_full, node_first = node + node_low, node + inside0 * node_low
        NDH[m] = NODE_DAMPING / node_full
        ND[m, 0] = node_first
        for p in range(1, PLANES):
            ND[m, p] = node_full
        for t in range(7):
            for p in range(PLANES):
                S[m, POS[t], p] = src[m, t, :, p, :]
        packs = list(packs)
        for s in range(2):
            for n, t in enumerate(SHARED):
                for p in range(PLANES):
                    packs[n] = packs[n] + ln.pack(S[m, POS[t], p], s, (m * 2 + s) * 4 + p)
            for n, (f_, g_) in enumerate([(full[t], first[t]) for t in SHARED] + [(node_full, node_first)]):
                packs[3] = packs[3] + ln.pack(f_, s, (m * 2 + s) * 4 + n)
                packs[4] = packs[4] + ln.pack(g_, s, (m * 2 + s) * 4 + n)
        return tuple(packs)

    packs = lax.fori_loop(0, macros, prepare, (zero,) * 5)
    for u in range(5):
        G0[row, u] = packs[u]

    pl.semaphore_wait(
        barrier, 2 * (side - 1) + 1 + jnp.where(has_up, 1, 0) + jnp.where(has_down, 1, 0)
    )
    gi.first()
    g0.first()

    def vertical(direction, source, target, sems, i):
        step = 1 - 2 * direction
        return pltpu.make_async_remote_copy(
            src_ref=source,
            dst_ref=target,
            send_sem=sems.at[i, direction, 0],
            recv_sem=sems.at[i, direction, 1],
            device_id=(dom, k + step),
            device_id_type=MESH,
        )

    pending = []

    def push(direction, source, target, sems, i):
        copy = vertical(direction, source, target, sems, i)
        able = has_down if direction else has_up
        pending.append((copy, able))

        @pl.when(able)
        def _():
            copy.start()

        return copy

    def pull(direction, source, target, sems, i):
        copy = vertical(direction, source, target, sems, i)

        @pl.when(has_up if direction else has_down)
        def _():
            copy.wait_recv()

    @pl.when(jnp.logical_not(has_down))
    def _():
        SB[...] = jnp.zeros_like(SB)
        RB[...] = jnp.zeros_like(RB)
        NB[...] = jnp.zeros_like(NB)
        for i in range(4):
            HR[i, 0] = zero

    @pl.when(jnp.logical_not(has_up))
    def _():
        SA[...] = jnp.zeros_like(SA)
        RA[...] = jnp.zeros_like(RA)
        NA[...] = jnp.zeros_like(NA)
        for i in range(4):
            HR[i, 1] = zero

    s_up = (0, S.at[:, :, PLANES - 1], SB, bsem, 0)
    s_down = (1, S.at[:, 0:3, 0], SA, bsem, 0)
    push(*s_up)
    push(*s_down)

    def inverse(m, t, p):
        if p == 0 and t in FLAT_TYPES:
            return INV0[m, POS[t]]
        return INVH[m, POS[t]]

    def start_private(m, carry):
        for t in PRIVATE:
            for p in range(PLANES):
                EF[m, POS[t], p + 1] = inverse(m, t, p) * S[m, POS[t], p]
        return carry

    lax.fori_loop(0, macros, start_private, 0)
    gi.second()
    g0.second()
    gi.third()
    gi.finish()

    def place(r, carry):
        c_ = r // (side * side)
        a_ = (r // side) % side
        b_ = r % side
        natural = jnp.where(c_ == 0, a_ * side + b_, b_ * side + a_) * CORES + c_
        ODS[pl.ds(natural, 1), :] = GI[r, 1:2, :]
        return carry

    ODS[...] = jnp.full(ODS.shape, -1, jnp.int32)
    lax.fori_loop(0, nd_dev, place, 0)
    slots = od_v.shape[1]
    owners = jnp.transpose(ODS[...])[0:slots]
    number = lax.broadcasted_iota(jnp.int32, owners.shape, 0) + 1

    def look(j, carry):
        e = od_s[0, j]
        c_ = e % CORES
        z_ = e // (CORES * side)
        y_ = (e // CORES) % side
        r = c_ * side * side + jnp.where(c_ == 0, z_ * side + y_, y_ * side + z_)
        GRS[pl.ds(j, 1), :] = GI[r, 0:1, :]
        hit = jnp.where(owners == e, number, 0)
        JS[pl.ds(j, 1), :] = jnp.max(hit, axis=0, keepdims=True)
        return carry

    lax.fori_loop(0, slots, look, 0)
    group, place_of = GRS[...], JS[...]
    device = lax.broadcasted_iota(jnp.int32, group.shape, 1)
    c_ = device % CORES
    z_ = device // (CORES * side)
    y_ = (device // CORES) % side
    rows = (c_ * side * side + jnp.where(c_ == 0, z_ * side + y_, y_ * side + z_))
    mine = jnp.max(jnp.where(device == dom, group, -2), axis=1, keepdims=True)
    mate = (group == mine) & (place_of > 0) & (device != dom)
    none = nd_dev * 32
    code = jnp.where(mate, rows * 32 + place_of - 1, none)
    found = jnp.zeros(group.shape, jnp.int32)
    for i in range(3):
        least = jnp.min(code, axis=1, keepdims=True)
        found = jnp.where(device == i, least, found)
        code = jnp.where(code == least, none, code)
    IDXV[...] = jnp.clip(found, 0, none)
    to_scalar = pltpu.make_async_copy(IDXV, IDXS, isem)
    to_scalar.start()
    to_scalar.wait()

    g0.third()
    g0.finish()

    def others(buf, units, m, p, s):
        j = (m * 2 + s) * 4 + p
        totals = [None] * len(units)
        for i in range(3):
            code = IDXS[j, i]
            r = jnp.clip(code // 32, 0, nd_dev)
            theirs = code % 32
            for n, u in enumerate(units):
                v = ln.unpack(buf[r, u], s, theirs)
                totals[n] = v if totals[n] is None else totals[n] + v
        return totals

    def others_diag(m, p, s):
        j = (m * 2 + s) * 4 + p
        totals = [None] * 4
        for i in range(3):
            code = IDXS[j, i]
            r = jnp.clip(code // 32, 0, nd_dev)
            theirs = code % 32
            low = theirs % 4
            v0 = G0[r, jnp.where(low == 0, 4, 3)]
            for n in range(4):
                v = ln.unpack(v0, s, theirs - low + n)
                totals[n] = v if totals[n] is None else totals[n] + v
        return totals

    def assembled(buf, units, m, p, values):
        for s in range(2):
            extra = others(buf, units, m, p, s)
            values = [jnp.where(ln.side(s), v + e, v) for v, e in zip(values, extra)]
        return values

    def start_shared(m, carry):
        up, down = carry
        for p in range(PLANES):
            values = assembled(G0, (0, 1, 2), m, p, [S[m, POS[t], p] for t in SHARED])
            diags = [INVS[m, n, p] for n in range(3)] + [ND[m, p]]
            for s in range(2):
                extra = others_diag(m, p, s)
                diags = [jnp.where(ln.side(s), v + e, v) for v, e in zip(diags, extra)]
            ND[m, p] = NODE_DAMPING / diags[3]
            for n, t in enumerate(SHARED):
                inv = EDGE_DAMPING / diags[n]
                INVS[m, n, p] = inv
                new = inv * values[n]
                EF[m, POS[t], p + 1] = new
                for s in range(2):
                    if p == PLANES - 1:
                        up = up + ln.pack(new, s, (m * 2 + s) * 4 + n)
                    if p == 0 and t == 1:
                        down = down + ln.pack(new, s, (m * 2 + s) * 4 + n)
        return up, down

    def send_sides(event, up, down, both=True):
        if both:
            HS[event, 0] = up
            push(0, HS.at[event, 0], HR.at[event, 0], hsem, event)
        HS[event, 1] = down
        push(1, HS.at[event, 1], HR.at[event, 1], hsem, event)

    def take_sides(event, both=True):
        if both:
            pull(0, HS.at[event, 0], HR.at[event, 0], hsem, event)
        pull(1, HS.at[event, 1], HR.at[event, 1], hsem, event)

    def replace(v, packed, m, n):
        for s in range(2):
            v = jnp.where(ln.side(s), ln.unpack(packed, s, (m * 2 + s) * 4 + n), v)
        return v

    up, down = lax.fori_loop(0, macros, start_shared, (zero, zero))
    send_sides(0, up, down)
    pull(*s_up)
    pull(*s_down)
    take_sides(0)

    def halo_edges(event, below, above, fresh):
        def body(m, carry):
            from_below, from_above = HR[event, 0], HR[event, 1]
            for t in range(7):
                v = INVH[m, POS[t]] * below[m, POS[t]]
                if not fresh:
                    v = EF[m, POS[t], 0] + v
                if t in SHARED:
                    v = replace(v, from_below, m, SHARED.index(t))
                EF[m, POS[t], 0] = v
            for t in FLAT_TYPES:
                v = INVH[m, POS[t]] * above[m, POS[t]]
                if not fresh:
                    v = EF[m, POS[t], PLANES + 1] + v
                if t in SHARED:
                    v = replace(v, from_above, m, 0)
                EF[m, POS[t], PLANES + 1] = v
            return carry

        lax.fori_loop(0, macros, body, 0)

    halo_edges(0, SB, SA, True)

    def operate(m, want_nodes, sink):
        mass = [MC[m, t] for t in range(7)]
        curl = [MC[m, 7 + f] for f in range(8)]
        w3b = w5b = w7b = None
        rb = None
        for z in range(-1, PLANES):
            u = {t: EF[m, POS[t], z + 1] for t in range(7)}
            n = {t: EF[m, POS[t], z + 2] for t in FLAT_TYPES}
            w3 = curl[3] * (u[2] + n[0] - u[4])
            w5 = curl[5] * (u[2] + n[1] - u[5])
            w7 = curl[7] * (u[2] + n[3] - u[6])
            if z == -1:
                w3, w5, w7 = inside0 * w3, inside0 * w5, inside0 * w7
            if z >= 0 or want_nodes:
                ay2 = ln.ay(u[2])
                w2 = curl[2] * (u[0] + ln.ax(u[2]) - u[4])
                w4 = curl[4] * (u[1] + ay2 - u[5])
                w6 = curl[6] * (u[3] + ln.ax(ay2) - u[6])

                def given(t):
                    return SB[m, POS[t]] if z < 0 else S[m, POS[t], z]

                r = {
                    2: given(2) - (mass[2] * u[2] + (w3 + w5 + w7) + ln.bx(w2 + ln.by(w6)) + ln.by(w4)),
                    4: given(4) - (mass[4] * u[4] - w2 - w3),
                    5: given(5) - (mass[5] * u[5] - w4 - w5),
                    6: given(6) - (mass[6] * u[6] - w6 - w7),
                }
                if z >= 0:
                    w0 = curl[0] * (u[0] + ln.ax(u[1]) - u[3])
                    w1 = curl[1] * (u[1] + ln.ay(u[0]) - u[3])
                    r[0] = given(0) - (mass[0] * u[0] + w0 + w2 + ln.by(w1) + w3b)
                    r[1] = given(1) - (mass[1] * u[1] + w1 + w4 + ln.bx(w0) + w5b)
                    r[3] = given(3) - (mass[3] * u[3] - w0 - w1 + w6 + w7b)
                    sink(z, r, rb)
                rb = r
            w3b, w5b, w7b = w3, w5, w7

    def node_stage(sweep):
        def body(m, pack):
            box = [pack]

            def sink(z, r, rb):
                total = ln.bx(r[0] + rb[4] + ln.by(r[3] + rb[6])) + ln.by(r[1] + rb[5]) + rb[2]
                own = ((r[0] + r[1]) + (r[2] + r[3])) + ((r[4] + r[5]) + r[6])
                node = total - own
                NR[sweep, m, z] = node
                for s in range(2):
                    box[0] = box[0] + ln.pack(node, s, (m * 2 + s) * 4 + z)

            operate(m, True, sink)
            return box[0]

        return lax.fori_loop(0, macros, body, zero)

    def node_round(sweep, gather, buf, corr, both):
        buf[row, 0] = node_stage(sweep)
        gather.first()
        n_up = (0, NR.at[sweep, :, PLANES - 1], NB, bsem, 1 + 2 * sweep)
        n_down = (1, NR.at[sweep, :, 0], NA.at[sweep], bsem, 1 + 2 * sweep)
        if both:
            push(*n_up)
        push(*n_down)
        gather.second()
        gather.third()
        gather.finish()

        def correct(m, carry):
            up_, down_ = carry
            for p in range(PLANES):
                (value,) = assembled(buf, (0,), m, p, [NR[sweep, m, p]])
                value = ND[m, p] * value
                corr[m, p + 1] = value
                for s in range(2):
                    if p == PLANES - 1:
                        up_ = up_ + ln.pack(value, s, (m * 2 + s) * 4)
                    if p == 0:
                        down_ = down_ + ln.pack(value, s, (m * 2 + s) * 4)
            return up_, down_

        up_, down_ = lax.fori_loop(0, macros, correct, (zero, zero))
        event = 1 + 2 * sweep
        send_sides(event, up_, down_, both)
        if both:
            pull(*n_up)
        pull(*n_down)
        take_sides(event, both)

        def halo(m, carry):
            if both:
                corr[m, 0] = replace(NDH[m] * NB[m], HR[event, 0], m, 0)
            corr[m, PLANES + 1] = replace(NDH[m] * NA[sweep, m], HR[event, 1], m, 0)
            return carry

        lax.fori_loop(0, macros, halo, 0)

    def raised(corr, m, z, t):
        dz = 0 if t in FLAT_TYPES else 1
        flat = {0: 0, 1: 1, 3: 3, 2: None, 4: 0, 5: 1, 6: 3}[t]
        v = corr[m, z + 1 + dz]
        if flat is not None:
            v = ahead[flat](v)
        return v - corr[m, z + 1]

    node_round(0, g1, G1, C1, True)

    def raise_all(m, carry):
        for t in range(7):
            for z in range(-1, PLANES):
                step = raised(C1, m, z, t)
                EF[m, POS[t], z + 1] = EF[m, POS[t], z + 1] + (inside0 * step if z < 0 else step)
        for t in FLAT_TYPES:
            EF[m, POS[t], PLANES + 1] = EF[m, POS[t], PLANES + 1] + raised(C1, m, PLANES, t)
        return carry

    lax.fori_loop(0, macros, raise_all, 0)

    def residual_stage(m, packs):
        box = list(packs)

        def sink(z, r, rb):
            for t in range(7):
                R[m, POS[t], z] = r[t]
            for n, t in enumerate(SHARED):
                for s in range(2):
                    box[n] = box[n] + ln.pack(r[t], s, (m * 2 + s) * 4 + z)

        operate(m, False, sink)
        return tuple(box)

    packs = lax.fori_loop(0, macros, residual_stage, (zero,) * 3)
    for u in range(3):
        G2[row, u] = packs[u]
    g2.first()
    r_up = (0, R.at[:, :, PLANES - 1], RB, bsem, 2)
    r_down = (1, R.at[:, 0:3, 0], RA, bsem, 2)
    push(*r_up)
    push(*r_down)

    def second_private(m, carry):
        for t in PRIVATE:
            for p in range(PLANES):
                EF[m, POS[t], p + 1] = EF[m, POS[t], p + 1] + inverse(m, t, p) * R[m, POS[t], p]
        return carry

    lax.fori_loop(0, macros, second_private, 0)
    g2.second()
    g2.third()
    g2.finish()

    def second_shared(m, carry):
        up, down = carry
        for p in range(PLANES):
            values = assembled(G2, (0, 1, 2), m, p, [R[m, POS[t], p] for t in SHARED])
            for n, t in enumerate(SHARED):
                new = EF[m, POS[t], p + 1] + INVS[m, n, p] * values[n]
                EF[m, POS[t], p + 1] = new
                for s in range(2):
                    if p == PLANES - 1:
                        up = up + ln.pack(new, s, (m * 2 + s) * 4 + n)
                    if p == 0 and t == 1:
                        down = down + ln.pack(new, s, (m * 2 + s) * 4 + n)
        return up, down

    up, down = lax.fori_loop(0, macros, second_shared, (zero, zero))
    send_sides(2, up, down)
    pull(*r_up)
    pull(*r_down)
    take_sides(2)
    halo_edges(2, RB, RA, False)
    node_round(1, g3, G3, C2, False)

    def finish(m, carry):
        for t in range(7):
            for z in range(PLANES):
                out_e[m, t, :, z, :] = EF[m, POS[t], z + 1] + raised(C2, m, z, t)
        for z in range(PLANES):
            out_p[m, :, z, :] = C1[m, z + 1] + C2[m, z + 1]
        return carry

    lax.fori_loop(0, macros, finish, 0)

    for gather in (gi, g0, g1, g2, g3):
        gather.drain()
    for copy, able in pending:
        @pl.when(able)
        def _(copy=copy):
            copy.wait_send()


def solution(mesh):
    n_dom, n_sub = mesh.shape["dom"], mesh.shape["sub"]
    side = 1
    while side * side * CORES < n_dom:
        side *= 2

    def local(source, zone_ids, kappa_table, mu_table, owner_dev, owner_group):
        macros, types, planes, cells = source.shape
        zones = kappa_table.shape[0]
        split = cells // 128
        src = source.reshape(macros, types, planes, split, 128)
        src = jnp.transpose(src, (0, 1, 3, 2, 4))
        zone = zone_ids.reshape(macros, split, 128)
        slots = owner_dev.shape[1]
        vmem = pl.BlockSpec(memory_space=pltpu.VMEM)
        smem = pl.BlockSpec(memory_space=pltpu.SMEM)

        def tiles(*lead):
            return pltpu.VMEM(lead + TILE, jnp.float32)

        m, rows = macros, n_dom + 1
        edge, pot = pl.pallas_call(
            functools.partial(kernel, side, n_sub, macros, zones),
            out_shape=(
                jax.ShapeDtypeStruct(src.shape, jnp.float32),
                jax.ShapeDtypeStruct((macros, split, planes, 128), jnp.float32),
            ),
            in_specs=[vmem, vmem, smem, vmem, vmem, smem, smem],
            out_specs=(vmem, vmem),
            scratch_shapes=[
                tiles(m, 7, 4), tiles(m, 7, 6), tiles(m, 7, 4),
                tiles(m, 7), tiles(m, 3), tiles(m, 7), tiles(m, 3),
                tiles(2, m, 4), tiles(m), tiles(2, m), tiles(m, 6), tiles(m, 6),
                tiles(m, 15), tiles(m, 7), tiles(m, 3), tiles(m, 3, 4), tiles(m), tiles(m), tiles(m, 4),
                tiles(rows, 5), tiles(rows, 1), tiles(rows, 3), tiles(rows, 1),
                pltpu.VMEM((n_dom,) + TILE, jnp.int32),
                tiles(4, 2), tiles(4, 2),
                pltpu.VMEM((128, 128), jnp.int32),
                pltpu.VMEM((slots, 128), jnp.int32),
                pltpu.VMEM((slots, 128), jnp.int32),
                pltpu.VMEM((slots, 128), jnp.int32),
                pltpu.SMEM((slots, 128), jnp.int32),
                pltpu.SemaphoreType.DMA((5, 3, 2, side)),
                pltpu.SemaphoreType.DMA((4, 2, 2)),
                pltpu.SemaphoreType.DMA((4, 2, 2)),
                pltpu.SemaphoreType.DMA,
            ],
            compiler_params=pltpu.CompilerParams(collective_id=0, has_side_effects=True),
        )(src, zone, owner_dev, owner_dev, owner_group, kappa_table.T, mu_table.T)

        def back(v):
            lead = v.shape[:-3]
            return jnp.swapaxes(v, -3, -2).reshape(lead + (planes, cells))

        return back(edge), back(pot)

    in_specs = (
        P("dom", None, "sub", None),
        P("dom", None),
        P(),
        P(),
        P("dom", None),
        P("dom", None),
    )
    out_specs = (P("dom", None, "sub", None), P("dom", "sub", None))
    return jax.shard_map(local, mesh=mesh, in_specs=in_specs, out_specs=out_specs, check_vma=False)
```

```python
import functools

import jax
import jax.numpy as jnp
from jax import lax
from jax.experimental import pallas as pl
from jax.experimental.pallas import tpu as pltpu
from jax.sharding import PartitionSpec as P

MESH = pl.DeviceIdType.MESH
LAT = 32
PLANES = 4
CORES = 2
EDGE_DAMPING = 0.6
NODE_DAMPING = 0.8
POS = {0: 0, 1: 1, 3: 2, 2: 3, 4: 4, 5: 5, 6: 6}
FLAT_TYPES = (0, 1, 3)
SHARED = (1, 2, 5)
PRIVATE = (0, 3, 4, 6)
TILE = (8, 128)


class Lanes:
    def __init__(self):
        self.lane = lax.broadcasted_iota(jnp.int32, TILE, 1)
        self.sub = lax.broadcasted_iota(jnp.int32, TILE, 0)
        self.x = self.lane & (LAT - 1)
        self.left = self.x == 0
        self.right = self.x == LAT - 1
        self.last_y = (self.sub == 7) & (self.lane >= 96)
        self.first_y = (self.sub == 0) & (self.lane < 32)

    def side(self, s):
        return self.right if s else self.left

    def ax(self, v):
        return jnp.where(self.right, 0.0, pltpu.roll(v, 127, 1))

    def bx(self, v):
        return jnp.where(self.left, 0.0, pltpu.roll(v, 1, 1))

    def ay(self, v):
        r = pltpu.roll(v, 96, 1)
        r = jnp.where(self.lane < 96, r, pltpu.roll(r, 7, 0))
        return jnp.where(self.last_y, 0.0, r)

    def by(self, v):
        r = pltpu.roll(v, 32, 1)
        r = jnp.where(self.lane >= 32, r, pltpu.roll(r, 1, 0))
        return jnp.where(self.first_y, 0.0, r)

    def pack(self, v, s, idx):
        return pltpu.roll(jnp.where(self.side(s), v, jnp.zeros_like(v)), (idx - s * (LAT - 1)) & 127, 1)

    def unpack(self, v, s, idx):
        return pltpu.roll(v, (s * (LAT - 1) - idx) & 127, 1)


def near_first(side):
    return sorted(range(1, side), key=lambda i: min(i, side - i))


def run_second(gathers):
    for i in [0] + near_first(gathers[0].side):
        for gather in gathers:
            gather.step(i)
    for gather in gathers:
        gather.second_done()


class Gather:
    def __init__(self, buf, sems, me, side):
        self.buf, self.sems = buf, sems
        self.side = side
        self.core, self.a, self.b, self.k, self.dev = me
        self.sent = []

    def row(self):
        return (self.core * self.side + self.a) * self.side + self.b

    def line(self, core, a):
        return self.buf.at[pl.ds((core * self.side + a) * self.side, self.side)]

    def copy(self, stage, i, ref, target):
        return pltpu.make_async_remote_copy(
            src_ref=ref,
            dst_ref=ref,
            send_sem=self.sems.at[stage, 0, i],
            recv_sem=self.sems.at[stage, 1, i],
            device_id=target,
            device_id_type=MESH,
        )

    def send(self, stage, i, ref, target):
        copy = self.copy(stage, i, ref, target)
        copy.start()
        self.sent.append(copy)

    def arrived(self, stage, i, ref):
        self.copy(stage, i, ref, self.dev(self.core, self.a, self.b)).wait_recv()

    def first(self):
        ref = self.buf.at[self.row()]
        for i in range(1, self.side):
            self.send(0, i, ref, self.dev(self.core, self.a, (self.b + i) % self.side))

    def forward(self, row):
        ref = self.buf.at[row]
        for i in range(1, self.side):
            self.copy(1, i, ref, self.dev(self.core, (self.a + i) % self.side, self.b)).start()

    def step(self, i):
        row = (self.core * self.side + self.a) * self.side + (self.b - i + self.side) % self.side
        if i:
            self.arrived(0, i, self.buf.at[row])
        self.forward(row)

    def second_done(self):
        ref = self.line(self.core, self.a)
        for i in range(1, self.side):
            self.sent.append(self.copy(1, i, ref, self.dev(self.core, self.a, self.b)))
        self.send(2, 0, ref, self.dev(1 - self.core, self.b, self.a))

    def second(self):
        run_second([self])

    def third(self):
        for i in near_first(self.side):
            ref = self.line(self.core, (self.a - i + self.side) % self.side)
            self.arrived(1, i, ref)
            self.send(2, i, ref, self.dev(1 - self.core, self.b, self.a))

    def finish(self):
        for i in range(self.side):
            self.arrived(2, i, self.line(1 - self.core, (self.b - i + self.side) % self.side))

    def drain(self):
        for copy in self.sent:
            copy.wait_send()


def kernel(
    side, n_sub, macros, zones,
    src, zone, od_s, od_v, og_v, kappa, mu,
    out_e, out_p,
    S, EF, R, SB, SA, RB, RA, NR, NB, NA, C1, C2,
    MC, INVH, INV0, INVS, NDH, DIAG, DSUM, ZS, ND,
    G0, G1, G2, G3, GI, HS, HR,
    SRC, ODS, OD2, GRS, JS, IDXV, IDXS,
    gsem, bsem, hsem, isem, lsem,
):
    dom = lax.axis_index("dom")
    k = lax.axis_index("sub")
    core = dom % CORES
    zc = dom // (CORES * side)
    yc = (dom // CORES) % side
    a = jnp.where(core == 0, zc, yc)
    b = jnp.where(core == 0, yc, zc)

    def dev(core_, a_, b_):
        z_ = jnp.where(core_ == 0, a_, b_)
        y_ = jnp.where(core_ == 0, b_, a_)
        return ((z_ * side + y_) * CORES + core_, k)

    me = (core, a, b, k, dev)
    barrier = pltpu.get_barrier_semaphore()

    def greet(target):
        pl.semaphore_signal(barrier, inc=1, device_id=target, device_id_type=MESH)

    for i in range(1, side):
        greet(dev(core, a, (b + i) % side))
        greet(dev(core, (a + i) % side, b))
    greet(dev(1 - core, b, a))
    has_up = k < n_sub - 1
    has_down = k > 0

    @pl.when(has_up)
    def _():
        greet((dom, k + 1))

    @pl.when(has_down)
    def _():
        greet((dom, k - 1))

    load = pltpu.make_async_copy(src, SRC, lsem)
    load.start()
    ln = Lanes()
    ahead = {0: ln.ax, 1: ln.ay, 3: lambda v: ln.ax(ln.ay(v))}
    behind = {0: ln.bx, 1: ln.by, 3: lambda v: ln.bx(ln.by(v))}
    zero = jnp.zeros(TILE, jnp.float32)
    inside0 = jnp.where(has_down, 1.0, 0.0)

    nd_dev = side * side * CORES
    for buf in (G0, G1, G2, G3):
        for u in range(buf.shape[1]):
            buf[nd_dev, u] = zero

    gi = Gather(GI, gsem.at[4], me, side)
    g0 = Gather(G0, gsem.at[0], me, side)
    g1 = Gather(G1, gsem.at[1], me, side)
    g2 = Gather(G2, gsem.at[2], me, side)
    g3 = Gather(G3, gsem.at[3], me, side)
    row = gi.row()

    GI[nd_dev] = jnp.full(TILE, zones, jnp.int32)
    IDXV[0:1, 0 : og_v.shape[1]] = og_v[...]
    IDXV[1:2, :] = jnp.full((1, 128), -1, jnp.int32)
    IDXV[1:2, 0 : od_v.shape[1]] = od_v[...]
    upper = lax.broadcasted_iota(jnp.int32, (1, 128), 1) & 31 >= 16
    zone_pack = jnp.zeros(TILE, jnp.int32)
    for m in range(macros):
        zid = zone[:, m, :]
        ZS[m] = zid
        zone_pack = zone_pack + ln.pack(zid, 0, m * 4) + ln.pack(jnp.full(TILE, zones, jnp.int32), 0, m * 4 + 1)
        zone_pack = zone_pack + ln.pack(zid, 1, m * 4 + 2) + ln.pack(pltpu.roll(zid, 1, 1), 1, m * 4 + 3)
    GI[row] = zone_pack
    for n in range(2):
        v = IDXV[n : n + 1, :]
        GI[row, 2 * n : 2 * n + 1, :] = jnp.where(upper, pltpu.roll(v, 16, 1), zone_pack[2 * n : 2 * n + 1])
        GI[row, 2 * n + 1 : 2 * n + 2, :] = jnp.where(upper, v, zone_pack[2 * n + 1 : 2 * n + 2])

    def load_source(m, packs):
        packs = list(packs)
        for t in range(7):
            for p in range(PLANES):
                v = SRC[m, t, :, p, :]
                S[m, POS[t], p] = v
                if t in SHARED:
                    n = SHARED.index(t)
                    for s in range(2):
                        packs[n] = packs[n] + ln.pack(v, s, (m * 2 + s) * 4 + p)
        return tuple(packs)

    load.wait()
    packs = lax.fori_loop(0, macros, load_source, (zero,) * 3)
    for u in range(3):
        G0[row, u] = packs[u]

    def prepare(m, carry):
        zid = ZS[m]
        mass, curl = [zero] * 7, [zero] * 8
        for zz in range(zones):
            hit = zid == zz
            mass = [jnp.where(hit, kappa[t, zz], v) for t, v in enumerate(mass)]
            curl = [jnp.where(hit, mu[f, zz], v) for f, v in enumerate(curl)]
        for t in range(7):
            MC[m, t] = mass[t]
        for f in range(8):
            MC[m, 7 + f] = curl[f]
        diag = {
            0: mass[0] + curl[0] + curl[2] + behind[1](curl[1]),
            1: mass[1] + curl[1] + curl[4] + behind[0](curl[0]),
            2: mass[2] + curl[3] + curl[5] + curl[7] + behind[0](curl[2]) + behind[1](curl[4]) + behind[3](curl[6]),
            3: mass[3] + curl[0] + curl[1] + curl[6],
            4: mass[4] + curl[2] + curl[3],
            5: mass[5] + curl[4] + curl[5],
            6: mass[6] + curl[6] + curl[7],
        }
        low = {0: curl[3], 1: curl[5], 3: curl[7]}
        node = functools.reduce(lambda p, q: p + q, mass) + behind[0](mass[0]) + behind[1](mass[1]) + behind[3](mass[3])
        node_low = mass[2] + behind[0](mass[4]) + behind[1](mass[5]) + behind[3](mass[6])
        full = {t: diag[t] + low[t] if t in low else diag[t] for t in range(7)}
        first = {t: diag[t] + inside0 * low[t] if t in low else diag[t] for t in range(7)}
        for t in range(7):
            INVH[m, POS[t]] = EDGE_DAMPING / full[t]
        for n, t in enumerate(FLAT_TYPES):
            INV0[m, n] = EDGE_DAMPING / first[t]
        node_full, node_first = node + node_low, node + inside0 * node_low
        NDH[m] = NODE_DAMPING / node_full
        for n, t in enumerate(SHARED):
            DIAG[m, 0, n] = first[t]
            DIAG[m, 1, n] = full[t]
        DIAG[m, 0, 3] = node_first
        DIAG[m, 1, 3] = node_full
        return carry

    pl.semaphore_wait(
        barrier, 2 * (side - 1) + 1 + jnp.where(has_up, 1, 0) + jnp.where(has_down, 1, 0)
    )
    gi.first()
    g0.first()

    def vertical(direction, source, target, sems, i):
        step = 1 - 2 * direction
        return pltpu.make_async_remote_copy(
            src_ref=source,
            dst_ref=target,
            send_sem=sems.at[i, direction, 0],
            recv_sem=sems.at[i, direction, 1],
            device_id=(dom, k + step),
            device_id_type=MESH,
        )

    pending = []

    def push(direction, source, target, sems, i):
        copy = vertical(direction, source, target, sems, i)
        able = has_down if direction else has_up
        pending.append((copy, able))

        @pl.when(able)
        def _():
            copy.start()

        return copy

    def pull(direction, source, target, sems, i):
        copy = vertical(direction, source, target, sems, i)

        @pl.when(has_up if direction else has_down)
        def _():
            copy.wait_recv()

    @pl.when(jnp.logical_not(has_down))
    def _():
        SB[...] = jnp.zeros_like(SB)
        RB[...] = jnp.zeros_like(RB)
        NB[...] = jnp.zeros_like(NB)
        for i in range(4):
            HR[i, 0] = zero

    @pl.when(jnp.logical_not(has_up))
    def _():
        SA[...] = jnp.zeros_like(SA)
        RA[...] = jnp.zeros_like(RA)
        NA[...] = jnp.zeros_like(NA)
        for i in range(4):
            HR[i, 1] = zero

    s_up = (0, S.at[:, :, PLANES - 1], SB, bsem, 0)
    s_down = (1, S.at[:, 0:3, 0], SA, bsem, 0)
    push(*s_up)
    push(*s_down)

    def inverse(m, t, p):
        if p == 0 and t in FLAT_TYPES:
            return INV0[m, POS[t]]
        return INVH[m, POS[t]]

    def start_private(m, carry):
        for t in PRIVATE:
            for p in range(PLANES):
                EF[m, POS[t], p + 1] = inverse(m, t, p) * S[m, POS[t], p]
        return carry

    lax.fori_loop(0, macros, prepare, 0)
    lax.fori_loop(0, macros, start_private, 0)
    run_second([gi])
    run_second([g0])
    gi.third()
    gi.finish()

    slots = od_v.shape[1]
    bits = side.bit_length() - 1

    def row_of(device):
        c_ = device & (CORES - 1)
        z_ = device >> (1 + bits)
        y_ = (device >> 1) & (side - 1)
        return (c_ << (2 * bits)) + jnp.where(c_ == 0, (z_ << bits) + y_, (y_ << bits) + z_)

    ODS[...] = jnp.full(ODS.shape, -1, jnp.int32)
    OD2[...] = jnp.full(ODS.shape, -1, jnp.int32)
    for device in range(nd_dev):
        c_, z_, y_ = device % CORES, device // (CORES * side), device // CORES % side
        r = c_ * side * side + (y_ * side + z_ if c_ else z_ * side + y_)
        ODS[device : device + 1, :] = GI[r, 2:3, :]
        OD2[device : device + 1, :] = GI[r, 3:4, :]
    upper_all = lax.broadcasted_iota(jnp.int32, ODS.shape, 1) & 31 >= 16
    ODS[...] = jnp.where(upper_all, OD2[...], pltpu.roll(ODS[...], 112, 1))
    owners = jnp.transpose(ODS[...])[0:slots]
    number = lax.broadcasted_iota(jnp.int32, owners.shape, 0) + 1

    def look(block, carry):
        for jj in range(8):
            j = block * 8 + jj
            e = od_s[0, j]
            two = GI[row_of(e), 0:2, :]
            GRS[pl.ds(j, 1), :] = jnp.where(upper, two[1:2], pltpu.roll(two[0:1], 112, 1))
            JS[pl.ds(j, 1), :] = jnp.max(jnp.where(owners == e, number, 0), axis=0, keepdims=True)
        return carry

    lax.fori_loop(0, slots // 8, look, 0)
    group, place_of = GRS[...], JS[...]
    device = lax.broadcasted_iota(jnp.int32, group.shape, 1)
    slot = lax.broadcasted_iota(jnp.int32, group.shape, 0)
    rows = row_of(device)
    mine = jnp.max(jnp.where(device == dom, group, -2), axis=1, keepdims=True)
    mate = (group == mine) & (place_of > 0) & (device != dom)
    none = nd_dev * 32
    code = jnp.where(mate, rows * 32 + place_of - 1, none)
    found = jnp.zeros(group.shape, jnp.int32)
    for i in range(3):
        least = jnp.min(code, axis=1, keepdims=True)
        theirs = least & 31
        low = theirs & 3
        found = jnp.where(device == i, jnp.clip(least >> 5, 0, nd_dev), found)
        found = jnp.where(device == 4 + i, (((slot >> 2) & 1) * (LAT - 1) - theirs) & 127, found)
        found = jnp.where(device == 8 + i, (slot - (theirs >> 2) * 2) & 127, found)
        found = jnp.where(device == 12 + i, low, found)
        code = jnp.where(code == least, none, code)
    IDXV[...] = found
    to_scalar = pltpu.make_async_copy(IDXV, IDXS, isem)
    to_scalar.start()
    to_scalar.wait()

    def mate_row(j, i):
        return jnp.clip(IDXS[j, i], 0, nd_dev)

    def fetch(block, carry):
        own, left, inner = [list(c) for c in carry]
        for jj in range(4):
            j = block * 4 + jj
            here = ln.x == j
            for i in range(3):
                v = GI[mate_row(j, i)]
                turn = IDXS[j, 8 + i]
                own[i] = jnp.where(here, pltpu.roll(v, turn, 1), own[i])
                left[i] = jnp.where(here, pltpu.roll(v, (turn - 1) & 127, 1), left[i])
                inner[i] = jnp.where(here, jnp.where(IDXS[j, 12 + i] == 0, inside0, 1.0), inner[i])
        return tuple(own), tuple(left), tuple(inner)

    izero = jnp.full(TILE, zones, jnp.int32)
    own, left, inner = lax.fori_loop(0, slots // 4, fetch, ((izero,) * 3, (izero,) * 3, (zero,) * 3))
    sums = [zero] * 4
    for i in range(3):
        mass = {t: zero for t in range(7)}
        curl = {f: zero for f in (1, 3, 4, 5, 7)}
        mass_x = {t: zero for t in (0, 3, 4, 6)}
        curl_x = {f: zero for f in (0, 2, 6)}
        for zz in range(zones):
            hit, hit_x = own[i] == zz, left[i] == zz
            mass = {t: jnp.where(hit, kappa[t, zz], v) for t, v in mass.items()}
            curl = {f: jnp.where(hit, mu[f, zz], v) for f, v in curl.items()}
            mass_x = {t: jnp.where(hit_x, kappa[t, zz], v) for t, v in mass_x.items()}
            curl_x = {f: jnp.where(hit_x, mu[f, zz], v) for f, v in curl_x.items()}
        sums[0] = sums[0] + mass[1] + curl[1] + curl[4] + curl_x[0] + inner[i] * curl[5]
        sums[1] = sums[1] + mass[2] + curl[3] + curl[5] + curl[7] + curl_x[2] + ln.by(curl[4] + curl_x[6])
        sums[2] = sums[2] + mass[5] + curl[4] + curl[5]
        sums[3] = sums[3] + functools.reduce(lambda p, q: p + q, [mass[t] for t in range(7)]) + mass_x[0]
        sums[3] = sums[3] + ln.by(mass[1] + mass_x[3])
        sums[3] = sums[3] + inner[i] * (mass[2] + mass_x[4] + ln.by(mass[5] + mass_x[6]))
    for n in range(4):
        DSUM[n] = sums[n]

    def invert(m, carry):
        for n in range(4):
            extra = DSUM[n]
            for p in range(PLANES):
                v = DIAG[m, 1 if p else 0, n]
                for s in range(2):
                    v = jnp.where(ln.side(s), v + ln.unpack(extra, s, (m * 2 + s) * 4 + p), v)
                if n < 3:
                    INVS[m, n, p] = EDGE_DAMPING / v
                else:
                    ND[m, p] = NODE_DAMPING / v
        return carry

    lax.fori_loop(0, macros, invert, 0)

    g0.third()
    g0.finish()

    def others(buf, units, m, p, s):
        j = (m * 2 + s) * 4 + p
        totals = [None] * len(units)
        for i in range(3):
            r, turn = mate_row(j, i), IDXS[j, 4 + i]
            for n, u in enumerate(units):
                v = pltpu.roll(buf[r, u], turn, 1)
                totals[n] = v if totals[n] is None else totals[n] + v
        return totals

    def assembled(buf, units, m, p, values):
        for s in range(2):
            extra = others(buf, units, m, p, s)
            values = [jnp.where(ln.side(s), v + e, v) for v, e in zip(values, extra)]
        return values

    def start_shared(m, carry):
        up, down = carry
        for p in range(PLANES):
            values = assembled(G0, (0, 1, 2), m, p, [S[m, POS[t], p] for t in SHARED])
            for n, t in enumerate(SHARED):
                new = INVS[m, n, p] * values[n]
                EF[m, POS[t], p + 1] = new
                for s in range(2):
                    if p == PLANES - 1:
                        up = up + ln.pack(new, s, (m * 2 + s) * 4 + n)
                    if p == 0 and t == 1:
                        down = down + ln.pack(new, s, (m * 2 + s) * 4 + n)
        return up, down

    def send_sides(event, up, down, both=True):
        if both:
            HS[event, 0] = up
            push(0, HS.at[event, 0], HR.at[event, 0], hsem, event)
        HS[event, 1] = down
        push(1, HS.at[event, 1], HR.at[event, 1], hsem, event)

    def take_sides(event, both=True):
        if both:
            pull(0, HS.at[event, 0], HR.at[event, 0], hsem, event)
        pull(1, HS.at[event, 1], HR.at[event, 1], hsem, event)

    def replace(v, packed, m, n):
        for s in range(2):
            v = jnp.where(ln.side(s), ln.unpack(packed, s, (m * 2 + s) * 4 + n), v)
        return v

    up, down = lax.fori_loop(0, macros, start_shared, (zero, zero))
    send_sides(0, up, down)
    pull(*s_up)
    pull(*s_down)
    take_sides(0)

    def halo_edges(event, below, above, fresh):
        def body(m, carry):
            from_below, from_above = HR[event, 0], HR[event, 1]
            for t in range(7):
                v = INVH[m, POS[t]] * below[m, POS[t]]
                if not fresh:
                    v = EF[m, POS[t], 0] + v
                if t in SHARED:
                    v = replace(v, from_below, m, SHARED.index(t))
                EF[m, POS[t], 0] = v
            for t in FLAT_TYPES:
                v = INVH[m, POS[t]] * above[m, POS[t]]
                if not fresh:
                    v = EF[m, POS[t], PLANES + 1] + v
                if t in SHARED:
                    v = replace(v, from_above, m, 0)
                EF[m, POS[t], PLANES + 1] = v
            return carry

        lax.fori_loop(0, macros, body, 0)

    halo_edges(0, SB, SA, True)

    def operate(m, want_nodes, sink):
        mass = [MC[m, t] for t in range(7)]
        curl = [MC[m, 7 + f] for f in range(8)]
        w3b = w5b = w7b = None
        rb = None
        for z in range(-1, PLANES):
            u = {t: EF[m, POS[t], z + 1] for t in range(7)}
            n = {t: EF[m, POS[t], z + 2] for t in FLAT_TYPES}
            w3 = curl[3] * (u[2] + n[0] - u[4])
            w5 = curl[5] * (u[2] + n[1] - u[5])
            w7 = curl[7] * (u[2] + n[3] - u[6])
            if z == -1:
                w3, w5, w7 = inside0 * w3, inside0 * w5, inside0 * w7
            if z >= 0 or want_nodes:
                ay2 = ln.ay(u[2])
                w2 = curl[2] * (u[0] + ln.ax(u[2]) - u[4])
                w4 = curl[4] * (u[1] + ay2 - u[5])
                w6 = curl[6] * (u[3] + ln.ax(ay2) - u[6])

                def given(t):
                    return SB[m, POS[t]] if z < 0 else S[m, POS[t], z]

                r = {
                    2: given(2) - (mass[2] * u[2] + (w3 + w5 + w7) + ln.bx(w2 + ln.by(w6)) + ln.by(w4)),
                    4: given(4) - (mass[4] * u[4] - w2 - w3),
                    5: given(5) - (mass[5] * u[5] - w4 - w5),
                    6: given(6) - (mass[6] * u[6] - w6 - w7),
                }
                if z >= 0:
                    w0 = curl[0] * (u[0] + ln.ax(u[1]) - u[3])
                    w1 = curl[1] * (u[1] + ln.ay(u[0]) - u[3])
                    r[0] = given(0) - (mass[0] * u[0] + w0 + w2 + ln.by(w1) + w3b)
                    r[1] = given(1) - (mass[1] * u[1] + w1 + w4 + ln.bx(w0) + w5b)
                    r[3] = given(3) - (mass[3] * u[3] - w0 - w1 + w6 + w7b)
                    sink(z, r, rb)
                rb = r
            w3b, w5b, w7b = w3, w5, w7

    def node_stage(sweep):
        def body(m, pack):
            box = [pack]

            def sink(z, r, rb):
                total = ln.bx(r[0] + rb[4] + ln.by(r[3] + rb[6])) + ln.by(r[1] + rb[5]) + rb[2]
                own = ((r[0] + r[1]) + (r[2] + r[3])) + ((r[4] + r[5]) + r[6])
                node = total - own
                NR[sweep, m, z] = node
                for s in range(2):
                    box[0] = box[0] + ln.pack(node, s, (m * 2 + s) * 4 + z)

            operate(m, True, sink)
            return box[0]

        return lax.fori_loop(0, macros, body, zero)

    def node_round(sweep, gather, buf, corr, both):
        buf[row, 0] = node_stage(sweep)
        gather.first()
        n_up = (0, NR.at[sweep, :, PLANES - 1], NB, bsem, 1 + 2 * sweep)
        n_down = (1, NR.at[sweep, :, 0], NA.at[sweep], bsem, 1 + 2 * sweep)
        if both:
            push(*n_up)
        push(*n_down)
        gather.second()
        gather.third()
        gather.finish()

        def correct(m, carry):
            up_, down_ = carry
            for p in range(PLANES):
                (value,) = assembled(buf, (0,), m, p, [NR[sweep, m, p]])
                value = ND[m, p] * value
                corr[m, p + 1] = value
                for s in range(2):
                    if p == PLANES - 1:
                        up_ = up_ + ln.pack(value, s, (m * 2 + s) * 4)
                    if p == 0:
                        down_ = down_ + ln.pack(value, s, (m * 2 + s) * 4)
            return up_, down_

        up_, down_ = lax.fori_loop(0, macros, correct, (zero, zero))
        event = 1 + 2 * sweep
        send_sides(event, up_, down_, both)
        if both:
            pull(*n_up)
        pull(*n_down)
        take_sides(event, both)

        def halo(m, carry):
            if both:
                corr[m, 0] = replace(NDH[m] * NB[m], HR[event, 0], m, 0)
            corr[m, PLANES + 1] = replace(NDH[m] * NA[sweep, m], HR[event, 1], m, 0)
            return carry

        lax.fori_loop(0, macros, halo, 0)

    def raised(corr, m, z, t):
        dz = 0 if t in FLAT_TYPES else 1
        flat = {0: 0, 1: 1, 3: 3, 2: None, 4: 0, 5: 1, 6: 3}[t]
        v = corr[m, z + 1 + dz]
        if flat is not None:
            v = ahead[flat](v)
        return v - corr[m, z + 1]

    node_round(0, g1, G1, C1, True)

    def raise_all(m, carry):
        for t in range(7):
            for z in range(-1, PLANES):
                step = raised(C1, m, z, t)
                EF[m, POS[t], z + 1] = EF[m, POS[t], z + 1] + (inside0 * step if z < 0 else step)
        for t in FLAT_TYPES:
            EF[m, POS[t], PLANES + 1] = EF[m, POS[t], PLANES + 1] + raised(C1, m, PLANES, t)
        return carry

    lax.fori_loop(0, macros, raise_all, 0)

    def residual_stage(m, packs):
        box = list(packs)

        def sink(z, r, rb):
            for t in range(7):
                R[m, POS[t], z] = r[t]
            for n, t in enumerate(SHARED):
                for s in range(2):
                    box[n] = box[n] + ln.pack(r[t], s, (m * 2 + s) * 4 + z)

        operate(m, False, sink)
        return tuple(box)

    packs = lax.fori_loop(0, macros, residual_stage, (zero,) * 3)
    for u in range(3):
        G2[row, u] = packs[u]
    g2.first()
    r_up = (0, R.at[:, :, PLANES - 1], RB, bsem, 2)
    r_down = (1, R.at[:, 0:3, 0], RA, bsem, 2)
    push(*r_up)
    push(*r_down)

    def second_private(m, carry):
        for t in PRIVATE:
            for p in range(PLANES):
                EF[m, POS[t], p + 1] = EF[m, POS[t], p + 1] + inverse(m, t, p) * R[m, POS[t], p]
        return carry

    lax.fori_loop(0, macros, second_private, 0)
    g2.second()
    g2.third()
    g2.finish()

    def second_shared(m, carry):
        up, down = carry
        for p in range(PLANES):
            values = assembled(G2, (0, 1, 2), m, p, [R[m, POS[t], p] for t in SHARED])
            for n, t in enumerate(SHARED):
                new = EF[m, POS[t], p + 1] + INVS[m, n, p] * values[n]
                EF[m, POS[t], p + 1] = new
                for s in range(2):
                    if p == PLANES - 1:
                        up = up + ln.pack(new, s, (m * 2 + s) * 4 + n)
                    if p == 0 and t == 1:
                        down = down + ln.pack(new, s, (m * 2 + s) * 4 + n)
        return up, down

    up, down = lax.fori_loop(0, macros, second_shared, (zero, zero))
    send_sides(2, up, down)
    pull(*r_up)
    pull(*r_down)
    take_sides(2)
    halo_edges(2, RB, RA, False)
    node_round(1, g3, G3, C2, False)

    def finish(m, carry):
        for t in range(7):
            for z in range(PLANES):
                out_e[m, t, :, z, :] = EF[m, POS[t], z + 1] + raised(C2, m, z, t)
        for z in range(PLANES):
            out_p[m, :, z, :] = C1[m, z + 1] + C2[m, z + 1]
        return carry

    lax.fori_loop(0, macros, finish, 0)

    for gather in (gi, g0, g1, g2, g3):
        gather.drain()
    for copy, able in pending:
        @pl.when(able)
        def _(copy=copy):
            copy.wait_send()


def solution(mesh):
    n_dom, n_sub = mesh.shape["dom"], mesh.shape["sub"]
    side = 1
    while side * side * CORES < n_dom:
        side *= 2

    def local(source, zone_ids, kappa_table, mu_table, owner_dev, owner_group):
        macros, types, planes, cells = source.shape
        zones = kappa_table.shape[0]
        split = cells // 128
        src = source.reshape(macros, types, planes, split, 128)
        src = jnp.transpose(src, (0, 1, 3, 2, 4))
        zone = jnp.transpose(zone_ids.reshape(macros, split, 128), (1, 0, 2))
        slots = owner_dev.shape[1]
        vmem = pl.BlockSpec(memory_space=pltpu.VMEM)
        smem = pl.BlockSpec(memory_space=pltpu.SMEM)

        def tiles(*lead):
            return pltpu.VMEM(lead + TILE, jnp.float32)

        m, rows = macros, n_dom + 1
        edge, pot = pl.pallas_call(
            functools.partial(kernel, side, n_sub, macros, zones),
            out_shape=(
                jax.ShapeDtypeStruct(src.shape, jnp.float32),
                jax.ShapeDtypeStruct((macros, split, planes, 128), jnp.float32),
            ),
            in_specs=[pl.BlockSpec(memory_space=pl.ANY), vmem, smem, vmem, vmem, smem, smem],
            out_specs=(vmem, vmem),
            scratch_shapes=[
                tiles(m, 7, 4), tiles(m, 7, 6), tiles(m, 7, 4),
                tiles(m, 7), tiles(m, 3), tiles(m, 7), tiles(m, 3),
                tiles(2, m, 4), tiles(m), tiles(2, m), tiles(m, 6), tiles(m, 6),
                tiles(m, 15), tiles(m, 7), tiles(m, 3), tiles(m, 3, 4), tiles(m), tiles(m, 2, 4), tiles(4),
                pltpu.VMEM((m,) + TILE, jnp.int32), tiles(m, 4),
                tiles(rows, 3), tiles(rows, 1), tiles(rows, 3), tiles(rows, 1),
                pltpu.VMEM((rows,) + TILE, jnp.int32),
                tiles(4, 2), tiles(4, 2),
                pltpu.VMEM((macros, types, split, planes, 128), jnp.float32),
                pltpu.VMEM((128, 128), jnp.int32),
                pltpu.VMEM((128, 128), jnp.int32),
                pltpu.VMEM((slots, 128), jnp.int32),
                pltpu.VMEM((slots, 128), jnp.int32),
                pltpu.VMEM((slots, 128), jnp.int32),
                pltpu.SMEM((slots, 128), jnp.int32),
                pltpu.SemaphoreType.DMA((5, 3, 2, side)),
                pltpu.SemaphoreType.DMA((4, 2, 2)),
                pltpu.SemaphoreType.DMA((4, 2, 2)),
                pltpu.SemaphoreType.DMA,
                pltpu.SemaphoreType.DMA,
            ],
            compiler_params=pltpu.CompilerParams(collective_id=0, has_side_effects=True),
        )(src, zone, owner_dev, owner_dev, owner_group, kappa_table.T, mu_table.T)

        def back(v):
            lead = v.shape[:-3]
            return jnp.swapaxes(v, -3, -2).reshape(lead + (planes, cells))

        return back(edge), back(pot)

    in_specs = (
        P("dom", None, "sub", None),
        P("dom", None),
        P(),
        P(),
        P("dom", None),
        P("dom", None),
    )
    out_specs = (P("dom", None, "sub", None), P("dom", "sub", None))
    return jax.shard_map(local, mesh=mesh, in_specs=in_specs, out_specs=out_specs, check_vma=False)
```

```python
import functools

import jax
import jax.numpy as jnp
from jax import lax
from jax.experimental import pallas as pl
from jax.experimental.pallas import tpu as pltpu
from jax.sharding import PartitionSpec as P

MESH = pl.DeviceIdType.MESH
LAT = 32
PLANES = 4
CORES = 2
EDGE_DAMPING = 0.6
NODE_DAMPING = 0.8
POS = {0: 0, 1: 1, 3: 2, 2: 3, 4: 4, 5: 5, 6: 6}
FLAT_TYPES = (0, 1, 3)
SHARED = (1, 2, 5)
PRIVATE = (0, 3, 4, 6)
TILE = (8, 128)


class Lanes:
    def __init__(self):
        self.lane = lax.broadcasted_iota(jnp.int32, TILE, 1)
        self.sub = lax.broadcasted_iota(jnp.int32, TILE, 0)
        self.x = self.lane & (LAT - 1)
        self.left = self.x == 0
        self.right = self.x == LAT - 1
        self.last_y = (self.sub == 7) & (self.lane >= 96)
        self.first_y = (self.sub == 0) & (self.lane < 32)

    def side(self, s):
        return self.right if s else self.left

    def ax(self, v):
        return jnp.where(self.right, 0.0, pltpu.roll(v, 127, 1))

    def bx(self, v):
        return jnp.where(self.left, 0.0, pltpu.roll(v, 1, 1))

    def ay(self, v):
        r = pltpu.roll(v, 96, 1)
        r = jnp.where(self.lane < 96, r, pltpu.roll(r, 7, 0))
        return jnp.where(self.last_y, 0.0, r)

    def by(self, v):
        r = pltpu.roll(v, 32, 1)
        r = jnp.where(self.lane >= 32, r, pltpu.roll(r, 1, 0))
        return jnp.where(self.first_y, 0.0, r)

    def pack(self, v, s, idx):
        return pltpu.roll(jnp.where(self.side(s), v, jnp.zeros_like(v)), (idx - s * (LAT - 1)) & 127, 1)

    def unpack(self, v, s, idx):
        return pltpu.roll(v, (s * (LAT - 1) - idx) & 127, 1)


def near_first(side):
    return sorted(range(1, side), key=lambda i: min(i, side - i))


def run_second(gathers, together=0):
    order = near_first(gathers[0].side)
    for i in order[:together]:
        for gather in gathers:
            gather.step(i)
    for gather in gathers:
        for i in order[together:]:
            gather.step(i)
        gather.second_done()


class Gather:
    def __init__(self, buf, sems, me, side):
        self.buf, self.sems = buf, sems
        self.side = side
        self.core, self.a, self.b, self.k, self.dev = me
        self.sent = []

    def row(self):
        return (self.core * self.side + self.a) * self.side + self.b

    def line(self, core, a):
        return self.buf.at[pl.ds((core * self.side + a) * self.side, self.side)]

    def copy(self, stage, i, ref, target):
        return pltpu.make_async_remote_copy(
            src_ref=ref,
            dst_ref=ref,
            send_sem=self.sems.at[stage, 0, i],
            recv_sem=self.sems.at[stage, 1, i],
            device_id=target,
            device_id_type=MESH,
        )

    def send(self, stage, i, ref, target):
        copy = self.copy(stage, i, ref, target)
        copy.start()
        self.sent.append(copy)

    def arrived(self, stage, i, ref):
        self.copy(stage, i, ref, self.dev(self.core, self.a, self.b)).wait_recv()

    def first(self):
        ref = self.buf.at[self.row()]
        for i in range(1, self.side):
            self.send(0, i, ref, self.dev(self.core, self.a, (self.b + i) % self.side))

    def forward(self, row):
        ref = self.buf.at[row]
        for i in range(1, self.side):
            self.copy(1, i, ref, self.dev(self.core, (self.a + i) % self.side, self.b)).start()

    def step(self, i):
        row = (self.core * self.side + self.a) * self.side + (self.b - i + self.side) % self.side
        if i:
            self.arrived(0, i, self.buf.at[row])
        self.forward(row)

    def second_done(self):
        ref = self.line(self.core, self.a)
        for i in range(1, self.side):
            self.sent.append(self.copy(1, i, ref, self.dev(self.core, self.a, self.b)))
        self.send(2, 0, ref, self.dev(1 - self.core, self.b, self.a))

    def second(self):
        self.step(0)
        run_second([self])

    def third(self):
        for i in near_first(self.side):
            ref = self.line(self.core, (self.a - i + self.side) % self.side)
            self.arrived(1, i, ref)
            self.send(2, i, ref, self.dev(1 - self.core, self.b, self.a))

    def finish(self):
        for i in range(self.side):
            self.arrived(2, i, self.line(1 - self.core, (self.b - i + self.side) % self.side))

    def drain(self):
        for copy in self.sent:
            copy.wait_send()


def kernel(
    side, n_sub, macros, zones,
    src, zone, od_s, od_v, og_v, kappa, mu,
    out_e, out_p,
    S, EF, R, SB, SA, RB, RA, NR, NB, NA, C1, C2,
    MC, INVH, INV0, INVP, NDH, ND0, EP, ZS,
    G0, G1, G2, G3, GI, HS, HR,
    SRC, ODS, OD2, GRS, JS, IDXV, IDXS,
    gsem, bsem, hsem, isem, lsem,
):
    dom = lax.axis_index("dom")
    k = lax.axis_index("sub")
    core = dom % CORES
    zc = dom // (CORES * side)
    yc = (dom // CORES) % side
    a = jnp.where(core == 0, zc, yc)
    b = jnp.where(core == 0, yc, zc)

    def dev(core_, a_, b_):
        z_ = jnp.where(core_ == 0, a_, b_)
        y_ = jnp.where(core_ == 0, b_, a_)
        return ((z_ * side + y_) * CORES + core_, k)

    me = (core, a, b, k, dev)
    barrier = pltpu.get_barrier_semaphore()

    def greet(target):
        pl.semaphore_signal(barrier, inc=1, device_id=target, device_id_type=MESH)

    for i in range(1, side):
        greet(dev(core, a, (b + i) % side))
        greet(dev(core, (a + i) % side, b))
    greet(dev(1 - core, b, a))
    has_up = k < n_sub - 1
    has_down = k > 0

    @pl.when(has_up)
    def _():
        greet((dom, k + 1))

    @pl.when(has_down)
    def _():
        greet((dom, k - 1))

    load = pltpu.make_async_copy(src, SRC, lsem)
    load.start()
    ln = Lanes()
    ahead = {0: ln.ax, 1: ln.ay, 3: lambda v: ln.ax(ln.ay(v))}
    behind = {0: ln.bx, 1: ln.by, 3: lambda v: ln.bx(ln.by(v))}
    zero = jnp.zeros(TILE, jnp.float32)
    inside0 = jnp.where(has_down, 1.0, 0.0)

    nd_dev = side * side * CORES
    for buf in (G0, G1, G2, G3):
        for u in range(buf.shape[1]):
            buf[nd_dev, u] = zero

    gi = Gather(GI, gsem.at[4], me, side)
    g0 = Gather(G0, gsem.at[0], me, side)
    g1 = Gather(G1, gsem.at[1], me, side)
    g2 = Gather(G2, gsem.at[2], me, side)
    g3 = Gather(G3, gsem.at[3], me, side)
    row = gi.row()

    GI[nd_dev] = jnp.full(TILE, zones, jnp.int32)
    IDXV[0:1, 0 : og_v.shape[1]] = og_v[...]
    IDXV[1:2, :] = jnp.full((1, 128), -1, jnp.int32)
    IDXV[1:2, 0 : od_v.shape[1]] = od_v[...]
    upper = lax.broadcasted_iota(jnp.int32, (1, 128), 1) & 31 >= 16
    zone_pack = jnp.zeros(TILE, jnp.int32)
    for m in range(macros):
        zid = zone[:, m, :]
        ZS[m] = zid
        zone_pack = zone_pack + ln.pack(zid, 0, m * 4) + ln.pack(jnp.full(TILE, zones, jnp.int32), 0, m * 4 + 1)
        zone_pack = zone_pack + ln.pack(zid, 1, m * 4 + 2) + ln.pack(pltpu.roll(zid, 1, 1), 1, m * 4 + 3)
    GI[row] = zone_pack
    for n in range(2):
        v = IDXV[n : n + 1, :]
        GI[row, 2 * n : 2 * n + 1, :] = jnp.where(upper, pltpu.roll(v, 16, 1), zone_pack[2 * n : 2 * n + 1])
        GI[row, 2 * n + 1 : 2 * n + 2, :] = jnp.where(upper, v, zone_pack[2 * n + 1 : 2 * n + 2])

    def load_source(m, packs):
        packs = list(packs)
        for t in range(7):
            for p in range(PLANES):
                v = SRC[m, t, :, p, :]
                S[m, POS[t], p] = v
                if t in SHARED:
                    n = SHARED.index(t)
                    for s in range(2):
                        packs[n] = packs[n] + ln.pack(v, s, (m * 2 + s) * 4 + p)
        return tuple(packs)

    load.wait()
    packs = lax.fori_loop(0, macros, load_source, (zero,) * 3)
    for u in range(3):
        G0[row, u] = packs[u]

    def prepare(m, packs):
        zid = ZS[m]
        mass, curl = [zero] * 7, [zero] * 8
        for zz in range(zones):
            hit = zid == zz
            mass = [jnp.where(hit, kappa[t, zz], v) for t, v in enumerate(mass)]
            curl = [jnp.where(hit, mu[f, zz], v) for f, v in enumerate(curl)]
        for t in range(7):
            MC[m, t] = mass[t]
        for f in range(8):
            MC[m, 7 + f] = curl[f]
        diag = {
            0: mass[0] + curl[0] + curl[2] + behind[1](curl[1]),
            1: mass[1] + curl[1] + curl[4] + behind[0](curl[0]),
            2: mass[2] + curl[3] + curl[5] + curl[7] + behind[0](curl[2]) + behind[1](curl[4]) + behind[3](curl[6]),
            3: mass[3] + curl[0] + curl[1] + curl[6],
            4: mass[4] + curl[2] + curl[3],
            5: mass[5] + curl[4] + curl[5],
            6: mass[6] + curl[6] + curl[7],
        }
        low = {0: curl[3], 1: curl[5], 3: curl[7]}
        node = functools.reduce(lambda p, q: p + q, mass) + behind[0](mass[0]) + behind[1](mass[1]) + behind[3](mass[3])
        node_low = mass[2] + behind[0](mass[4]) + behind[1](mass[5]) + behind[3](mass[6])
        full = {t: diag[t] + low[t] if t in low else diag[t] for t in range(7)}
        first = {t: diag[t] + inside0 * low[t] if t in low else diag[t] for t in range(7)}
        for t in range(7):
            INVH[m, POS[t]] = EDGE_DAMPING / full[t]
        for n, t in enumerate(FLAT_TYPES):
            INV0[m, n] = EDGE_DAMPING / first[t]
        node_full, node_first = node + node_low, node + inside0 * node_low
        NDH[m] = NODE_DAMPING / node_full
        ND0[m] = NODE_DAMPING / node_first
        packs = list(packs)
        for n, (f_, g_) in enumerate([(full[t], first[t]) for t in SHARED] + [(node_full, node_first)]):
            for s in range(2):
                for p in range(PLANES):
                    packs[n] = packs[n] + ln.pack(f_ if p else g_, s, (m * 2 + s) * 4 + p)
        return tuple(packs)

    pl.semaphore_wait(
        barrier, 2 * (side - 1) + 1 + jnp.where(has_up, 1, 0) + jnp.where(has_down, 1, 0)
    )
    gi.first()
    g0.first()

    def vertical(direction, source, target, sems, i):
        step = 1 - 2 * direction
        return pltpu.make_async_remote_copy(
            src_ref=source,
            dst_ref=target,
            send_sem=sems.at[i, direction, 0],
            recv_sem=sems.at[i, direction, 1],
            device_id=(dom, k + step),
            device_id_type=MESH,
        )

    pending = []

    def push(direction, source, target, sems, i):
        copy = vertical(direction, source, target, sems, i)
        able = has_down if direction else has_up
        pending.append((copy, able))

        @pl.when(able)
        def _():
            copy.start()

        return copy

    def pull(direction, source, target, sems, i):
        copy = vertical(direction, source, target, sems, i)

        @pl.when(has_up if direction else has_down)
        def _():
            copy.wait_recv()

    @pl.when(jnp.logical_not(has_down))
    def _():
        SB[...] = jnp.zeros_like(SB)
        RB[...] = jnp.zeros_like(RB)
        NB[...] = jnp.zeros_like(NB)
        for i in range(4):
            for n in range(3):
                HR[i, 0, n] = zero

    @pl.when(jnp.logical_not(has_up))
    def _():
        SA[...] = jnp.zeros_like(SA)
        RA[...] = jnp.zeros_like(RA)
        NA[...] = jnp.zeros_like(NA)
        for i in range(4):
            for n in range(3):
                HR[i, 1, n] = zero

    s_up = (0, S.at[:, :, PLANES - 1], SB, bsem, 0)
    s_down = (1, S.at[:, 0:3, 0], SA, bsem, 0)
    push(*s_up)
    push(*s_down)

    def inverse(m, t, p):
        if p == 0 and t in FLAT_TYPES:
            return INV0[m, POS[t]]
        return INVH[m, POS[t]]

    def halo_edges(below, above, fresh):
        def body(m, carry):
            for t in range(7):
                v = INVH[m, POS[t]] * below[m, POS[t]]
                EF[m, POS[t], 0] = v if fresh else EF[m, POS[t], 0] + v
            for t in FLAT_TYPES:
                v = INVH[m, POS[t]] * above[m, POS[t]]
                EF[m, POS[t], PLANES + 1] = v if fresh else EF[m, POS[t], PLANES + 1] + v
            return carry

        lax.fori_loop(0, macros, body, 0)

    def start_all(m, carry):
        for t in range(7):
            for p in range(PLANES):
                EF[m, POS[t], p + 1] = inverse(m, t, p) * S[m, POS[t], p]
        return carry

    gi.step(0)
    g0.step(0)
    diag_sides = lax.fori_loop(0, macros, prepare, (zero,) * 4)
    for n in range(4):
        INVP[n] = diag_sides[n]
    run_second([gi, g0], 0)
    lax.fori_loop(0, macros, start_all, 0)
    pull(*s_up)
    pull(*s_down)
    halo_edges(SB, SA, True)
    gi.third()
    gi.finish()

    slots = od_v.shape[1]
    bits = side.bit_length() - 1

    def row_of(device):
        c_ = device & (CORES - 1)
        z_ = device >> (1 + bits)
        y_ = (device >> 1) & (side - 1)
        return (c_ << (2 * bits)) + jnp.where(c_ == 0, (z_ << bits) + y_, (y_ << bits) + z_)

    ODS[...] = jnp.full(ODS.shape, -1, jnp.int32)
    OD2[...] = jnp.full(ODS.shape, -1, jnp.int32)
    for device in range(nd_dev):
        c_, z_, y_ = device % CORES, device // (CORES * side), device // CORES % side
        r = c_ * side * side + (y_ * side + z_ if c_ else z_ * side + y_)
        ODS[device : device + 1, :] = GI[r, 2:3, :]
        OD2[device : device + 1, :] = GI[r, 3:4, :]
    upper_all = lax.broadcasted_iota(jnp.int32, ODS.shape, 1) & 31 >= 16
    ODS[...] = jnp.where(upper_all, OD2[...], pltpu.roll(ODS[...], 112, 1))
    owners = jnp.transpose(ODS[...])[0:slots]
    number = lax.broadcasted_iota(jnp.int32, owners.shape, 0) + 1

    def look(block, carry):
        for jj in range(8):
            j = block * 8 + jj
            e = od_s[0, j]
            two = GI[row_of(e), 0:2, :]
            GRS[pl.ds(j, 1), :] = jnp.where(upper, two[1:2], pltpu.roll(two[0:1], 112, 1))
            JS[pl.ds(j, 1), :] = jnp.max(jnp.where(owners == e, number, 0), axis=0, keepdims=True)
        return carry

    lax.fori_loop(0, slots // 8, look, 0)
    group, place_of = GRS[...], JS[...]
    device = lax.broadcasted_iota(jnp.int32, group.shape, 1)
    slot = lax.broadcasted_iota(jnp.int32, group.shape, 0)
    rows = row_of(device)
    mine = jnp.max(jnp.where(device == dom, group, -2), axis=1, keepdims=True)
    mate = (group == mine) & (place_of > 0) & (device != dom)
    none = nd_dev * 32
    code = jnp.where(mate, rows * 32 + place_of - 1, none)
    found = jnp.zeros(group.shape, jnp.int32)
    for i in range(3):
        least = jnp.min(code, axis=1, keepdims=True)
        theirs = least & 31
        low = theirs & 3
        found = jnp.where(device == i, jnp.clip(least >> 5, 0, nd_dev), found)
        found = jnp.where(device == 4 + i, (slot - theirs) & 127, found)
        found = jnp.where(device == 8 + i, (slot - (theirs >> 2) * 2) & 127, found)
        found = jnp.where(device == 12 + i, low, found)
        code = jnp.where(code == least, none, code)
    IDXV[...] = found
    to_scalar = pltpu.make_async_copy(IDXV, IDXS, isem)
    to_scalar.start()
    to_scalar.wait()

    def mate_row(j, i):
        return jnp.clip(IDXS[j, i], 0, nd_dev)

    def fetch(block, carry):
        own, left, inner = [list(c) for c in carry]
        for jj in range(4):
            j = block * 4 + jj
            here = ln.x == j
            for i in range(3):
                v = GI[mate_row(j, i)]
                turn = IDXS[j, 8 + i]
                own[i] = jnp.where(here, pltpu.roll(v, turn, 1), own[i])
                left[i] = jnp.where(here, pltpu.roll(v, (turn - 1) & 127, 1), left[i])
                inner[i] = jnp.where(here, jnp.where(IDXS[j, 12 + i] == 0, inside0, 1.0), inner[i])
        return tuple(own), tuple(left), tuple(inner)

    izero = jnp.full(TILE, zones, jnp.int32)
    own, left, inner = lax.fori_loop(0, slots // 4, fetch, ((izero,) * 3, (izero,) * 3, (zero,) * 3))
    sums = [zero] * 4
    for i in range(3):
        mass = {t: zero for t in range(7)}
        curl = {f: zero for f in (1, 3, 4, 5, 7)}
        mass_x = {t: zero for t in (0, 3, 4, 6)}
        curl_x = {f: zero for f in (0, 2, 6)}
        for zz in range(zones):
            hit, hit_x = own[i] == zz, left[i] == zz
            mass = {t: jnp.where(hit, kappa[t, zz], v) for t, v in mass.items()}
            curl = {f: jnp.where(hit, mu[f, zz], v) for f, v in curl.items()}
            mass_x = {t: jnp.where(hit_x, kappa[t, zz], v) for t, v in mass_x.items()}
            curl_x = {f: jnp.where(hit_x, mu[f, zz], v) for f, v in curl_x.items()}
        sums[0] = sums[0] + mass[1] + curl[1] + curl[4] + curl_x[0] + inner[i] * curl[5]
        sums[1] = sums[1] + mass[2] + curl[3] + curl[5] + curl[7] + curl_x[2] + ln.by(curl[4] + curl_x[6])
        sums[2] = sums[2] + mass[5] + curl[4] + curl[5]
        sums[3] = sums[3] + functools.reduce(lambda p, q: p + q, [mass[t] for t in range(7)]) + mass_x[0]
        sums[3] = sums[3] + ln.by(mass[1] + mass_x[3])
        sums[3] = sums[3] + inner[i] * (mass[2] + mass_x[4] + ln.by(mass[5] + mass_x[6]))
    for n in range(4):
        INVP[n] = (EDGE_DAMPING if n < 3 else NODE_DAMPING) / (INVP[n] + sums[n])

    g0.third()
    g0.finish()

    def mates(buf, units):
        def body(m, acc):
            acc = list(acc)
            for q in range(8):
                j = m * 8 + q
                here = ln.x == j
                totals = [None] * len(units)
                for i in range(3):
                    r, turn = mate_row(j, i), IDXS[j, 4 + i]
                    for n, u in enumerate(units):
                        v = pltpu.roll(buf[r, u], turn, 1)
                        totals[n] = v if totals[n] is None else totals[n] + v
                acc = [jnp.where(here, t, v) for t, v in zip(totals, acc)]
            return tuple(acc)

        return lax.fori_loop(0, macros, body, (zero,) * len(units))

    def sides_message(event, edges):
        last = 3 if edges else 1
        up_ = (0, HS.at[event, 0:last], HR.at[event, 0, 0:last], hsem, event)
        down_ = (1, HS.at[event, 0:1], HR.at[event, 1, 0:1], hsem, event)
        return up_, down_

    def replace(v, packed, m, p):
        for s in range(2):
            v = jnp.where(ln.side(s), ln.unpack(packed, s, (m * 2 + s) * 4 + p), v)
        return v

    def edge_sides(event, values):
        for n in range(3):
            HS[event, n] = values[n]
        up_, down_ = sides_message(event, True)
        push(*up_)
        push(*down_)

        def own(m, carry):
            for n, t in enumerate(SHARED):
                for p in range(PLANES):
                    EF[m, POS[t], p + 1] = replace(EF[m, POS[t], p + 1], HS[event, n], m, p)
            return carry

        lax.fori_loop(0, macros, own, 0)
        pull(*up_)
        pull(*down_)

        def halo(m, carry):
            for n, t in enumerate(SHARED):
                EF[m, POS[t], 0] = replace(EF[m, POS[t], 0], HR[event, 0, n], m, PLANES - 1)
            EF[m, POS[1], PLANES + 1] = replace(EF[m, POS[1], PLANES + 1], HR[event, 1, 0], m, 0)
            return carry

        lax.fori_loop(0, macros, halo, 0)

    extra = mates(G0, (0, 1, 2))
    edge_sides(0, [INVP[n] * (G0[row, n] + extra[n]) for n in range(3)])

    def operate(m, want_nodes, sink):
        mass = [MC[m, t] for t in range(7)]
        curl = [MC[m, 7 + f] for f in range(8)]
        w3b = w5b = w7b = None
        rb = None
        for z in range(-1, PLANES):
            u = {t: EF[m, POS[t], z + 1] for t in range(7)}
            n = {t: EF[m, POS[t], z + 2] for t in FLAT_TYPES}
            w3 = curl[3] * (u[2] + n[0] - u[4])
            w5 = curl[5] * (u[2] + n[1] - u[5])
            w7 = curl[7] * (u[2] + n[3] - u[6])
            if z == -1:
                w3, w5, w7 = inside0 * w3, inside0 * w5, inside0 * w7
            if z >= 0 or want_nodes:
                ay2 = ln.ay(u[2])
                w2 = curl[2] * (u[0] + ln.ax(u[2]) - u[4])
                w4 = curl[4] * (u[1] + ay2 - u[5])
                w6 = curl[6] * (u[3] + ln.ax(ay2) - u[6])

                def given(t):
                    return SB[m, POS[t]] if z < 0 else S[m, POS[t], z]

                r = {
                    2: given(2) - (mass[2] * u[2] + (w3 + w5 + w7) + ln.bx(w2 + ln.by(w6)) + ln.by(w4)),
                    4: given(4) - (mass[4] * u[4] - w2 - w3),
                    5: given(5) - (mass[5] * u[5] - w4 - w5),
                    6: given(6) - (mass[6] * u[6] - w6 - w7),
                }
                if z >= 0:
                    w0 = curl[0] * (u[0] + ln.ax(u[1]) - u[3])
                    w1 = curl[1] * (u[1] + ln.ay(u[0]) - u[3])
                    r[0] = given(0) - (mass[0] * u[0] + w0 + w2 + ln.by(w1) + w3b)
                    r[1] = given(1) - (mass[1] * u[1] + w1 + w4 + ln.bx(w0) + w5b)
                    r[3] = given(3) - (mass[3] * u[3] - w0 - w1 + w6 + w7b)
                    sink(z, r, rb)
                rb = r
            w3b, w5b, w7b = w3, w5, w7

    def node_stage(sweep):
        def body(m, pack):
            box = [pack]

            def sink(z, r, rb):
                total = ln.bx(r[0] + rb[4] + ln.by(r[3] + rb[6])) + ln.by(r[1] + rb[5]) + rb[2]
                own = ((r[0] + r[1]) + (r[2] + r[3])) + ((r[4] + r[5]) + r[6])
                node = total - own
                NR[sweep, m, z] = node
                for s in range(2):
                    box[0] = box[0] + ln.pack(node, s, (m * 2 + s) * 4 + z)

            operate(m, True, sink)
            return box[0]

        return lax.fori_loop(0, macros, body, zero)

    def node_round(sweep, gather, buf, corr, both):
        buf[row, 0] = node_stage(sweep)
        gather.first()
        n_up = (0, NR.at[sweep, :, PLANES - 1], NB, bsem, 1 + 2 * sweep)
        n_down = (1, NR.at[sweep, :, 0], NA.at[sweep], bsem, 1 + 2 * sweep)
        if both:
            push(*n_up)
        push(*n_down)

        def interior(m, carry):
            for p in range(PLANES):
                corr[m, p + 1] = (NDH[m] if p else ND0[m]) * NR[sweep, m, p]
            return carry

        gather.second()
        lax.fori_loop(0, macros, interior, 0)
        if both:
            pull(*n_up)
        pull(*n_down)

        def halo(m, carry):
            if both:
                corr[m, 0] = NDH[m] * NB[m]
            corr[m, PLANES + 1] = NDH[m] * NA[sweep, m]
            return carry

        lax.fori_loop(0, macros, halo, 0)
        gather.third()
        gather.finish()
        (extra,) = mates(buf, (0,))
        event = 1 + 2 * sweep
        HS[event, 0] = INVP[3] * (buf[row, 0] + extra)
        up_, down_ = sides_message(event, False)
        if both:
            push(*up_)
        push(*down_)

        def own(m, carry):
            for p in range(PLANES):
                corr[m, p + 1] = replace(corr[m, p + 1], HS[event, 0], m, p)
            return carry

        lax.fori_loop(0, macros, own, 0)
        if both:
            pull(*up_)
        pull(*down_)

        def halo_sides(m, carry):
            if both:
                corr[m, 0] = replace(corr[m, 0], HR[event, 0, 0], m, PLANES - 1)
            corr[m, PLANES + 1] = replace(corr[m, PLANES + 1], HR[event, 1, 0], m, 0)
            return carry

        lax.fori_loop(0, macros, halo_sides, 0)

    def raised(corr, m, z, t):
        dz = 0 if t in FLAT_TYPES else 1
        flat = {0: 0, 1: 1, 3: 3, 2: None, 4: 0, 5: 1, 6: 3}[t]
        v = corr[m, z + 1 + dz]
        if flat is not None:
            v = ahead[flat](v)
        return v - corr[m, z + 1]

    node_round(0, g1, G1, C1, True)

    def raise_all(m, carry):
        for t in range(7):
            for z in range(-1, PLANES):
                step = raised(C1, m, z, t)
                EF[m, POS[t], z + 1] = EF[m, POS[t], z + 1] + (inside0 * step if z < 0 else step)
        for t in FLAT_TYPES:
            EF[m, POS[t], PLANES + 1] = EF[m, POS[t], PLANES + 1] + raised(C1, m, PLANES, t)
        return carry

    lax.fori_loop(0, macros, raise_all, 0)

    def residual_stage(m, packs):
        box = list(packs)

        def sink(z, r, rb):
            for t in range(7):
                R[m, POS[t], z] = r[t]
            for n, t in enumerate(SHARED):
                for s in range(2):
                    box[n] = box[n] + ln.pack(r[t], s, (m * 2 + s) * 4 + z)

        operate(m, False, sink)
        return tuple(box)

    packs = lax.fori_loop(0, macros, residual_stage, (zero,) * 3)
    for u in range(3):
        G2[row, u] = packs[u]
    g2.first()
    r_up = (0, R.at[:, :, PLANES - 1], RB, bsem, 2)
    r_down = (1, R.at[:, 0:3, 0], RA, bsem, 2)
    push(*r_up)
    push(*r_down)

    def second_all(m, packs):
        packs = list(packs)
        for t in range(7):
            for p in range(PLANES):
                v = EF[m, POS[t], p + 1]
                if t in SHARED:
                    n = SHARED.index(t)
                    for s in range(2):
                        packs[n] = packs[n] + ln.pack(v, s, (m * 2 + s) * 4 + p)
                EF[m, POS[t], p + 1] = v + inverse(m, t, p) * R[m, POS[t], p]
        return tuple(packs)

    g2.second()
    packs = lax.fori_loop(0, macros, second_all, (zero,) * 3)
    for n in range(3):
        EP[n] = packs[n]
    pull(*r_up)
    pull(*r_down)
    halo_edges(RB, RA, False)
    g2.third()
    g2.finish()
    extra = mates(G2, (0, 1, 2))
    edge_sides(2, [EP[n] + INVP[n] * (G2[row, n] + extra[n]) for n in range(3)])
    node_round(1, g3, G3, C2, False)

    def finish(m, carry):
        for t in range(7):
            for z in range(PLANES):
                out_e[m, t, :, z, :] = EF[m, POS[t], z + 1] + raised(C2, m, z, t)
        for z in range(PLANES):
            out_p[m, :, z, :] = C1[m, z + 1] + C2[m, z + 1]
        return carry

    lax.fori_loop(0, macros, finish, 0)

    for gather in (gi, g0, g1, g2, g3):
        gather.drain()
    for copy, able in pending:
        @pl.when(able)
        def _(copy=copy):
            copy.wait_send()


def solution(mesh):
    n_dom, n_sub = mesh.shape["dom"], mesh.shape["sub"]
    side = 1
    while side * side * CORES < n_dom:
        side *= 2

    def local(source, zone_ids, kappa_table, mu_table, owner_dev, owner_group):
        macros, types, planes, cells = source.shape
        zones = kappa_table.shape[0]
        split = cells // 128
        src = source.reshape(macros, types, planes, split, 128)
        src = jnp.transpose(src, (0, 1, 3, 2, 4))
        zone = jnp.transpose(zone_ids.reshape(macros, split, 128), (1, 0, 2))
        slots = owner_dev.shape[1]
        vmem = pl.BlockSpec(memory_space=pltpu.VMEM)
        smem = pl.BlockSpec(memory_space=pltpu.SMEM)

        def tiles(*lead):
            return pltpu.VMEM(lead + TILE, jnp.float32)

        m, rows = macros, n_dom + 1
        edge, pot = pl.pallas_call(
            functools.partial(kernel, side, n_sub, macros, zones),
            out_shape=(
                jax.ShapeDtypeStruct(src.shape, jnp.float32),
                jax.ShapeDtypeStruct((macros, split, planes, 128), jnp.float32),
            ),
            in_specs=[pl.BlockSpec(memory_space=pl.ANY), vmem, smem, vmem, vmem, smem, smem],
            out_specs=(vmem, vmem),
            scratch_shapes=[
                tiles(m, 7, 4), tiles(m, 7, 6), tiles(m, 7, 4),
                tiles(m, 7), tiles(m, 3), tiles(m, 7), tiles(m, 3),
                tiles(2, m, 4), tiles(m), tiles(2, m), tiles(m, 6), tiles(m, 6),
                tiles(m, 15), tiles(m, 7), tiles(m, 3), tiles(4), tiles(m), tiles(m), tiles(3),
                pltpu.VMEM((m,) + TILE, jnp.int32),
                tiles(rows, 3), tiles(rows, 1), tiles(rows, 3), tiles(rows, 1),
                pltpu.VMEM((rows,) + TILE, jnp.int32),
                tiles(4, 3), tiles(4, 2, 3),
                pltpu.VMEM((macros, types, split, planes, 128), jnp.float32),
                pltpu.VMEM((128, 128), jnp.int32),
                pltpu.VMEM((128, 128), jnp.int32),
                pltpu.VMEM((slots, 128), jnp.int32),
                pltpu.VMEM((slots, 128), jnp.int32),
                pltpu.VMEM((slots, 128), jnp.int32),
                pltpu.SMEM((slots, 128), jnp.int32),
                pltpu.SemaphoreType.DMA((5, 3, 2, side)),
                pltpu.SemaphoreType.DMA((4, 2, 2)),
                pltpu.SemaphoreType.DMA((4, 2, 2)),
                pltpu.SemaphoreType.DMA,
                pltpu.SemaphoreType.DMA,
            ],
            compiler_params=pltpu.CompilerParams(collective_id=0, has_side_effects=True),
        )(src, zone, owner_dev, owner_dev, owner_group, kappa_table.T, mu_table.T)

        def back(v):
            lead = v.shape[:-3]
            return jnp.swapaxes(v, -3, -2).reshape(lead + (planes, cells))

        return back(edge), back(pot)

    in_specs = (
        P("dom", None, "sub", None),
        P("dom", None),
        P(),
        P(),
        P("dom", None),
        P("dom", None),
    )
    out_specs = (P("dom", None, "sub", None), P("dom", "sub", None))
    return jax.shard_map(local, mesh=mesh, in_specs=in_specs, out_specs=out_specs, check_vma=False)
```
